32 devices in a mesh: groups: 2 (over x), panel: 16 (over z, y, core).
Axes of the slice: x: 2, y: 2, z: 4, core: 2. Of those that a mesh axis runs over, the one named last changes fastest.
Arguments:
- eig_vectors: bfloat16 [5120, 1024], P(('groups', 'panel')), parts along dimension 0, may hold values from -0.1875 to 0.1875
- eig_values: bfloat16 [5120], P(('groups', 'panel')), parts along dimension 0, may hold values from 0.19921875 to 5
- eig_count: int32 [16], P('groups'), parts along dimension 0, may hold values from 128 to 512, as said below
- snp_count: int32 [16], P('groups'), parts along dimension 0, may hold values from 512 to 1024
- zscores: bfloat16 [32, 8, 1024, 128], P(('groups', 'panel')), parts along dimension 0, may hold values from -6 to 6
- samples: bfloat16 [4096], P('groups'), parts along dimension 0, may hold values from 20 to 160
Outputs:
- covariance: float32 [9, 32, 8, 128, 128], P(None, ('groups', 'panel')), parts along dimension 1
The draws below stay inside these ranges and needn't reach their ends.
There are 2 independent parts, one for each index of `groups`. The reference program is written for one: setup_inputs(seed, part) draws one part's arguments, and reference() takes and returns one part's arrays. A program takes and returns all parts, laid end to end along the dimension named above; each array names one. Nothing has to cross between parts.
Inputs may be any that keep to these rules, and one draw needn't show every extreme that they name: `eig_count`: blocks 2m and 2m+1 hold 640 eigenvectors together, so every block group holds 2560; some block holds exactly 512.
All inputs are finite; a program needn't handle non-finite values.
Results may differ from the reference program's by a relative error of at most 0.0045.
Values may be sent and summed in bfloat16 or wider, within the bound.
A program may use at most 64 MiB of HBM per device.

```python
import math
import jax
import jax.numpy as jnp
from jax import lax

PW = 128
MB = 1024
KMAX = 512
KMEAN = 320
BLOCKS = 8
ROUNDS = 8
BG = 1
NP = 16
TRAITS = 2048
BPG = 8
GROUP_ROWS = 2560
EIGS = 2560
EIG_DEV = 160
N_PANEL = 16


def draw_eig_count(key, part):
    pair_count = BLOCKS // 2
    spread = KMAX - KMEAN
    key_left, key_right = jax.random.split(jax.random.fold_in(key, 17))
    offset_draw = jax.random.randint(key_left, (pair_count,), -spread, spread + 1)
    forced = jax.random.randint(key_right, (), 0, pair_count)
    offset_draw = jnp.where(jnp.arange(pair_count) == forced, spread, offset_draw)
    counts = jnp.stack([KMEAN + offset_draw, KMEAN - offset_draw], axis=1).reshape(BLOCKS)
    return counts.astype(jnp.int32)


def with_ends(result, stream_key, low, largest):
    longest = result.shape.index(max(result.shape))
    spots = []
    for shift in (0, 1):
        where = [jax.random.randint(jax.random.fold_in(stream_key, axis), (), 0, length) for axis, length in enumerate(result.shape)]
        where[longest] = (where[longest] + shift) % result.shape[longest]
        spots.append(tuple(where))
    return result.at[spots[0]].set(low).at[spots[1]].set(largest)


def steps_of(rng, extent, cuts, least, high):
    gain, own = 1.0, jax.random.fold_in(rng, 6)
    for axis_at, shards_of in cuts:
        draws = jnp.exp(jax.random.uniform(jax.random.fold_in(own, axis_at), (shards_of,), jnp.float32, least / len(cuts), high / len(cuts)))
        gain = gain * jnp.repeat(draws, extent[axis_at] // shards_of).reshape([-1 if axis == axis_at else 1 for axis in range(len(extent))])
    return gain


def noise(rng, extent, scale, reach, cuts=(), kind=jnp.bfloat16):
    entries = jax.random.normal(rng, extent, jnp.float32) * scale
    if len(cuts) > 0:
        entries = steps_of(rng, extent, cuts, -0.22, 0.18) * entries
    return jnp.clip(entries, min=-reach, max=reach).astype(kind)


def setup_inputs(seed: int = 0, part: int = 0) -> dict:
    key_of = jax.random.split(jax.random.key(seed), 7)
    part_keys = jax.random.split(jax.random.fold_in(key_of[6], part), 7)
    eig_vectors = noise(part_keys[0], (EIGS, MB), MB ** -0.5, 0.1875, ((0, 16),))
    eig_values = jnp.clip(jnp.exp(math.log(5.0) - 3.2227897 * jax.random.uniform(part_keys[1], (EIGS,), jnp.float32) ** steps_of(part_keys[1], (EIGS,), ((0, 16),), -0.2, 0.2)), 0.19921875, 5.0).astype(jnp.bfloat16)
    eig_count = draw_eig_count(jax.random.fold_in(jax.random.fold_in(key_of[6], part), 71), part)
    snp_count = with_ends(jax.random.randint(part_keys[3], (BLOCKS,), MB // 2, MB + 1), jax.random.fold_in(part_keys[3], 1), MB // 2, MB).astype(jnp.int32)
    zscores = noise(part_keys[4], (N_PANEL, BPG, MB, PW), 1.0, 6.0, ((0, 16),))
    samples = jnp.clip(jnp.exp(jax.random.uniform(part_keys[5], (TRAITS,), jnp.float32, math.log(20.0), math.log(160.0))), 20.0, 160.0).astype(jnp.bfloat16)
    return dict(eig_vectors=eig_vectors, eig_values=eig_values, eig_count=eig_count, snp_count=snp_count, zscores=zscores, samples=samples)


def project_blocks(vectors, counts, snps, scores):
    offsets = (jnp.cumsum(counts) - counts).astype(jnp.int32)
    row_total = vectors.shape[0]
    positions = jnp.arange(scores.shape[1], dtype=jnp.int32)
    kept = jnp.arange(KMAX, dtype=jnp.int32)

    def one_block(block_index, projected):
        start_row = offsets[block_index]
        live_count = counts[block_index]
        row_start = jnp.minimum(start_row, row_total - KMAX).astype(jnp.int32)
        eig_rows = lax.dynamic_slice_in_dim(vectors, row_start, KMAX, 0)
        block_scores = lax.dynamic_index_in_dim(scores, block_index, 0, keepdims=False)
        z_masked = jnp.where((positions < snps[block_index])[:, None], block_scores, jnp.zeros_like(block_scores))
        projection = jnp.dot(eig_rows, z_masked, preferred_element_type=jnp.float32).astype(jnp.bfloat16)
        row_index = row_start + kept
        keep_rows = (row_index >= start_row) & (row_index < start_row + live_count)
        previous = lax.dynamic_slice_in_dim(projected, row_start, KMAX, 0)
        merged = jnp.where(keep_rows[:, None], projection, previous)
        return lax.dynamic_update_slice_in_dim(projected, merged, row_start, 0)
    initial = jnp.zeros((row_total, scores.shape[2]), jnp.bfloat16)
    return lax.fori_loop(0, counts.shape[0], one_block, initial)

def reference(eig_vectors, eig_values, eig_count, snp_count, zscores, samples):
    vectors_all = eig_vectors.reshape(NP, BG, EIG_DEV, MB)
    values_all = eig_values.reshape(NP, BG, EIG_DEV)
    scores_all = zscores.reshape(NP, BG, BPG, MB, PW)
    scales = samples.astype(jnp.float32).reshape(NP, PW)
    kept = jnp.arange(KMAX, dtype=jnp.int32)
    group_results = []
    for group_index in range(BG):
        vectors = vectors_all[:, group_index].reshape(GROUP_ROWS, MB)
        values = values_all[:, group_index].reshape(GROUP_ROWS)
        counts = eig_count[group_index * BPG:(group_index + 1) * BPG]
        snps = snp_count[group_index * BPG:(group_index + 1) * BPG]
        scores = jnp.transpose(scores_all[:, group_index], (1, 2, 0, 3)).reshape(BPG, MB, NP * PW)
        projected = project_blocks(vectors, counts, snps, scores)
        weighted = (projected.astype(jnp.float32) / values.astype(jnp.float32)[:, None]).astype(jnp.bfloat16)
        weighted_wide = weighted.astype(jnp.float32).reshape(GROUP_ROWS, NP, PW)
        projected_wide = projected.astype(jnp.float32).reshape(GROUP_ROWS, NP, PW)
        offsets = (jnp.cumsum(counts) - counts).astype(jnp.int32)
        round_results = []
        for round_index in range(ROUNDS + 1):
            partner = jnp.roll(projected_wide, round_index, axis=1)
            partner_scale = jnp.roll(scales, round_index, axis=0)

            def block_gram(block_index):
                start_row = offsets[block_index]
                row_start = jnp.minimum(start_row, GROUP_ROWS - KMAX).astype(jnp.int32)
                row_index = row_start + kept
                keep_rows = (row_index >= start_row) & (row_index < start_row + counts[block_index])
                left_slab = lax.dynamic_slice_in_dim(weighted_wide, row_start, KMAX, 0)
                left_slab = jnp.where(keep_rows[:, None, None], left_slab, jnp.zeros_like(left_slab))
                right_slab = lax.dynamic_slice_in_dim(partner, row_start, KMAX, 0)
                gram = jnp.einsum('kpa,kpc->pac', left_slab, right_slab, precision=lax.Precision.HIGHEST)
                if round_index == 0:
                    gram = gram - counts[block_index].astype(jnp.float32) * jnp.eye(PW, dtype=jnp.float32)[None]
                return gram / jnp.sqrt(scales[:, :, None] * partner_scale[:, None, :])
            grams = lax.map(block_gram, jnp.arange(BPG, dtype=jnp.int32))
            round_results.append(jnp.transpose(grams, (1, 0, 2, 3)))
        group_results.append(jnp.stack(round_results))
    stacked = jnp.stack(group_results, axis=2)
    return stacked.reshape(ROUNDS + 1, NP * BG, BPG, PW, PW)
```

```python
import functools

import jax
import jax.numpy as jnp
from jax import lax
from jax.experimental import pallas as pl
from jax.experimental.pallas import tpu as pltpu
from jax.sharding import PartitionSpec as P

ROUNDS = 8
LIMIT = 56 * 1024 * 1024
EXCHANGE_LIMIT = 36 * 1024 * 1024


def place_masked(snps, scores, pair, store):
    width = scores.shape[-1]
    for side in range(2):
        block = 2 * pair + side
        rows = lax.broadcasted_iota(jnp.int32, scores.shape[-2:], 0)
        part = jnp.where(rows < snps[block], scores[side].astype(jnp.float32), 0.0)
        store[:, side * width : (side + 1) * width] = part.astype(jnp.bfloat16)


def project_rows(vectors, masked, first_count):
    both = jnp.dot(vectors, masked, preferred_element_type=jnp.float32)
    width = both.shape[1] // 2
    rows = lax.broadcasted_iota(jnp.int32, (both.shape[0], width), 0)
    return jnp.where(rows < first_count, both[:, :width], both[:, width:]).astype(jnp.bfloat16)


def project_kernel(counts, snps, vectors, scores, out, masked):
    pair = pl.program_id(0)
    place_masked(snps, scores.at[0], pair, masked)
    out[...] = project_rows(vectors[...], masked[...], counts[2 * pair])


def project(vectors, scores, counts, snps):
    row_total, depth = vectors.shape
    blocks, snp_rows, width = scores.shape[1:]
    pair_rows = 2 * row_total // blocks
    return pl.pallas_call(
        project_kernel,
        out_shape=jax.ShapeDtypeStruct((row_total, width), jnp.bfloat16),
        grid_spec=pltpu.PrefetchScalarGridSpec(
            num_scalar_prefetch=2,
            grid=(blocks // 2,),
            in_specs=[
                pl.BlockSpec((pair_rows, depth), lambda b, *_: (b, 0)),
                pl.BlockSpec((1, 2, snp_rows, width), lambda b, *_: (0, b, 0, 0)),
            ],
            out_specs=pl.BlockSpec((pair_rows, width), lambda b, *_: (b, 0)),
            scratch_shapes=[pltpu.VMEM((snp_rows, 2 * width), jnp.bfloat16)],
        ),
        compiler_params=pltpu.CompilerParams(vmem_limit_bytes=LIMIT),
    )(counts, snps, vectors, scores)


def gram_kernel(counts, slots, weighted, panels, scale, out):
    pair = pl.program_id(0)
    width = weighted.shape[1]
    left = weighted[...].astype(jnp.float32)
    rows = lax.broadcasted_iota(jnp.int32, left.shape, 0)
    first = rows < counts[2 * pair]
    left = jnp.concatenate([jnp.where(first, left, 0.0).T, jnp.where(first, 0.0, left).T], axis=0)
    left = left.astype(jnp.bfloat16)
    shape = (width, width)
    same = lax.broadcasted_iota(jnp.int32, shape, 0) == lax.broadcasted_iota(jnp.int32, shape, 1)
    for index in range(out.shape[0]):
        both = jnp.dot(left, panels[slots[index]], preferred_element_type=jnp.float32)
        for side in range(2):
            gram = both[side * width : (side + 1) * width]
            if index == 0:
                count = counts[2 * pair + side].astype(jnp.float32)
                gram = gram - jnp.where(same, count, 0.0)
            out[index, 0, side] = gram * scale[index]


def grams(weighted, panels, scale, slots, counts):
    blocks = counts.shape[0]
    rounds, width = scale.shape[:2]
    pair_rows = 2 * weighted.shape[0] // blocks
    return pl.pallas_call(
        gram_kernel,
        out_shape=jax.ShapeDtypeStruct((rounds, 1, blocks, width, width), jnp.float32),
        grid_spec=pltpu.PrefetchScalarGridSpec(
            num_scalar_prefetch=2,
            grid=(blocks // 2,),
            in_specs=[
                pl.BlockSpec((pair_rows, width), lambda b, *_: (b, 0)),
                pl.BlockSpec((panels.shape[0], pair_rows, width), lambda b, *_: (0, b, 0)),
                pl.BlockSpec(scale.shape, lambda b, *_: (0, 0, 0)),
            ],
            out_specs=pl.BlockSpec((rounds, 1, 2, width, width), lambda b, *_: (0, 0, b, 0, 0)),
        ),
        compiler_params=pltpu.CompilerParams(vmem_limit_bytes=LIMIT),
    )(counts, slots, weighted, panels, scale)


def exchange_kernel(counts, snps, own, own_values, scores, out, held, values, left, store, raw,
                    masked, here, load, send1, recv1, send2, recv2):
    line = lax.axis_size("panel") // 4
    me = lax.axis_index("panel")
    z = me // 4
    y = (me // 2) % 2
    k = me % 2
    piece = own.shape[0]
    pair_rows = 4 * piece
    parts = recv1.shape[1]
    part_rows = piece // (parts - 1)
    chunks = recv2.shape[1]
    top = line - 1
    inner = (z > 0) & (z < top)
    edge = (z == 0) | (z == top)
    up, down, across, beside = me + 4, me - 4, me + 2 - 4 * y, me + 1 - 2 * k
    skip = me + 8 - 16 * (z // 2)
    pending = []

    def order(plane, step):
        near = jnp.minimum(plane, top - plane)
        nearest = jnp.where(step > 2 * near, step, (near + (step + 1) // 2 * (1 - 2 * (step % 2))))
        return jnp.where(plane > top - plane, top - nearest, nearest)

    loads = []
    for step in range(line):
        pair = pl.ds(2 * order(z, step), 2)
        loads.append(
            pltpu.make_async_copy(scores.at[0, pair], raw.at[pl.ds(2 * step, 2)], load.at[step])
        )
    local = [
        pltpu.make_async_copy(own, store.at[pl.ds(me * piece, piece)], here.at[0]),
        pltpu.make_async_copy(own_values, values.at[me], here.at[1]),
    ]
    for copy in local + loads:
        copy.start()

    barrier = pltpu.get_barrier_semaphore()

    def greet(target):
        pl.semaphore_signal(
            barrier, inc=1, device_id={"panel": target}, device_id_type=pl.DeviceIdType.MESH
        )

    pl.when(z < top)(functools.partial(greet, up))
    pl.when(z > 0)(functools.partial(greet, down))
    for target in (across, beside, skip):
        greet(target)
    pl.semaphore_wait(barrier, jnp.where(inner, 5, 4))

    def start(condition, copy):
        if condition is None:
            copy.start()
        else:
            pl.when(condition)(copy.start)
        pending.append((condition, copy))

    def remote(source, target, send, recv, device):
        return pltpu.make_async_remote_copy(
            src_ref=source,
            dst_ref=target,
            send_sem=send,
            recv_sem=recv,
            device_id={"panel": device},
            device_id_type=pl.DeviceIdType.MESH,
        )

    def move1(source, part, way, target, first=False):
        sems = send1.at[way, source, part], recv1.at[source, part]
        if part == parts - 1:
            origin = own_values if first else values.at[source]
            return remote(origin, values.at[source], *sems, target)
        rows = pl.ds(source * piece + part * part_rows, part_rows)
        origin = own.at[pl.ds(part * part_rows, part_rows)] if first else store.at[rows]
        return remote(origin, store.at[rows], *sems, target)

    def arrive1(source, part):
        move1(source, part, 0, beside).wait_recv()

    def move2(source, chunk, way, target):
        block = held.at[source, pl.ds(chunk * pair_rows, pair_rows)]
        return remote(block, block, send2.at[way, source, chunk], recv2.at[source, chunk], target)

    def arrive2(source, chunk):
        move2(source, chunk, 0, beside).wait_recv()

    def both(a, b):
        return b if a is None else a & b

    def column(step, condition=None):
        plane = order(z, step)
        source = plane * 4 + y * 2 + k
        for part in range(parts):
            if condition is None:
                arrive1(source, part)
            else:
                pl.when(condition)(functools.partial(arrive1, source, part))
            start(both(condition, (plane < z) & (z < top)), move1(source, part, 0, up))
            start(both(condition, (plane > z) & (z > 0)), move1(source, part, 1, down))
            start(condition, move1(source, part, 2, across))
            start(condition, move1(source, part, 3, beside))

    def sideways(step):
        source = order(z, step) * 4 + 2 - 2 * y + k
        for part in range(parts):
            arrive1(source, part)
            start(None, move1(source, part, 3, beside))

    def mask(step):
        loads[step].wait()
        place_masked(snps, raw.at[pl.ds(2 * step, 2)], order(z, step), masked.at[step])

    def finish(step):
        plane = order(z, step)
        for source in (plane * 4 + y * 2 + 1 - k, plane * 4 + 2 - 2 * y + 1 - k):
            for part in range(parts):
                arrive1(source, part)
        rows = pl.ds(plane * pair_rows, pair_rows)
        held[me, rows] = project_rows(store[rows], masked[step], counts[2 * plane])
        start(z < top, move2(me, plane, 0, up))
        start(z >= 2, move2(me, plane, 1, skip))
        start(k == 0, move2(me, plane, 3, beside))
        weigh(plane)

    def weigh(index):
        rows = pl.ds(index * pair_rows, pair_rows)
        row = values[4 * index] + values[4 * index + 1]
        row = row + (values[4 * index + 2] + values[4 * index + 3])
        flat = held[me, rows].astype(jnp.float32).T / row
        first = lax.broadcasted_iota(jnp.int32, flat.shape, 1) < counts[2 * index]
        both = jnp.concatenate([jnp.where(first, flat, 0.0), jnp.where(first, 0.0, flat)], axis=0)
        left[index] = both.astype(jnp.bfloat16)

    def plane_behind(lag):
        return lax.rem(z - lag + line, line)

    def own_across(step):
        start(y == 0, move2(me, order(z, step), 2, across))

    def relay(step):
        for turn in range(2):
            lag = jnp.where(z == 0, 2 - turn, 1 + turn)
            plane = plane_behind(lag)
            source = plane * 4 + y * 2 + k
            chunk = order(plane, step)
            arrive2(source, chunk)
            start((lag == 1) & inner, move2(source, chunk, 0, up))
            start((lag == 2) & (z == 1), move2(source, chunk, 1, down))
            start((lag == 1) | (y == 1), move2(source, chunk, 2, across))
            start((lag == 1) | (k == 1), move2(source, chunk, 3, beside))

    cross = [plane_behind(lag + 1 - y) * 4 + (1 - y) * 2 + k for lag in range(2)]
    near = [plane_behind(lag) * 4 + y * 2 + k for lag in range(3)]
    swap = 1 - 2 * k

    def cross_over(step):
        for source in cross:
            chunk = order(source // 4, step)
            arrive2(source, chunk)
            start(None, move2(source, chunk, 3, beside))

    def gram(source, step, number, own_panel=False):
        chunk = order(source // 4, step)
        rows = pl.ds(chunk * pair_rows, pair_rows)
        both = jnp.dot(left[chunk], held[source, rows], preferred_element_type=jnp.float32)
        width = both.shape[1]
        for side in range(2):
            part = both[side * width : (side + 1) * width]
            if own_panel:
                shape = (width, width)
                across_rows = lax.broadcasted_iota(jnp.int32, shape, 0)
                same = across_rows == lax.broadcasted_iota(jnp.int32, shape, 1)
                count = counts[2 * chunk + side].astype(jnp.float32)
                part = part - jnp.where(same, count, 0.0)
            out[number, 0, 2 * chunk + side] = part

    def grams_near(step):
        for lag, source in enumerate(near):
            gram(source, step, 4 * lag, lag == 0)

    def grams_near_beside(step):
        for lag, source in enumerate(near):
            number = 4 * lag - swap

            @pl.when((number >= 0) & (number < out.shape[0]))
            def _():
                arrive2(source + swap, order(source // 4, step))
                gram(source + swap, step, number)

    def grams_cross(step):
        for lag, source in enumerate(cross):
            gram(source, step, 4 * lag + 2)

    def grams_cross_beside(step):
        for lag, source in enumerate(cross):
            arrive2(source + swap, order(source // 4, step))
            gram(source + swap, step, 4 * lag + 2 - swap)

    for part in range(parts):
        start(z < top, move1(me, part, 0, up, True))
        start(z > 0, move1(me, part, 1, down, True))
        start(None, move1(me, part, 2, across, True))
        start(None, move1(me, part, 3, beside, True))
    mask(0)
    for copy in local:
        copy.wait()
    column(1)
    column(2, inner)
    sideways(0)
    finish(0)
    mask(1)
    column(2, edge)
    column(3, inner)
    sideways(1)
    finish(1)
    mask(2)
    column(3, edge)
    mask(3)
    sideways(2)
    own_across(0)
    finish(2)
    relay(0)
    sideways(3)
    finish(3)
    own_across(1)
    relay(1)
    cross_over(0)
    grams_near(0)
    grams_near_beside(0)
    own_across(2)
    relay(2)
    cross_over(1)
    grams_cross(0)
    grams_cross_beside(0)
    grams_near(1)
    grams_near_beside(1)
    own_across(3)
    relay(3)
    cross_over(2)
    grams_cross(1)
    grams_cross_beside(1)
    grams_near(2)
    grams_near_beside(2)
    grams_near(3)
    grams_near_beside(3)
    grams_cross(2)
    cross_over(3)
    grams_cross_beside(2)
    grams_cross(3)
    grams_cross_beside(3)
    for condition, copy in pending:
        if condition is None:
            copy.wait_send()
        else:
            pl.when(condition)(copy.wait_send)


def exchange(vectors, values, counts, snps, scores):
    devices = lax.axis_size("panel")
    piece, depth = vectors.shape
    blocks, snp_rows, width = scores.shape[1:]
    row_total = devices * piece
    pair_rows = 4 * piece
    place = lax.rem(lax.axis_index("panel"), 4)
    lanes = jnp.arange(pair_rows, dtype=jnp.int32) // piece
    rider = jnp.where(lanes == place, jnp.tile(values.astype(jnp.float32), 4), 0.0)[None]
    parts = 3
    chunks = blocks // 2
    vmem = pl.BlockSpec(memory_space=pltpu.VMEM)
    smem = pl.BlockSpec(memory_space=pltpu.SMEM)
    anywhere = pl.BlockSpec(memory_space=pltpu.HBM)
    return pl.pallas_call(
        exchange_kernel,
        out_shape=jax.ShapeDtypeStruct((ROUNDS + 1, 1, blocks, width, width), jnp.float32),
        in_specs=[smem, smem, anywhere, anywhere, anywhere],
        out_specs=vmem,
        scratch_shapes=[
            pltpu.VMEM((devices, row_total, width), jnp.bfloat16),
            pltpu.VMEM((devices, 1, pair_rows), jnp.float32),
            pltpu.VMEM((chunks, 2 * width, pair_rows), jnp.bfloat16),
            pltpu.VMEM((row_total, depth), jnp.bfloat16),
            pltpu.VMEM((blocks, snp_rows, width), jnp.bfloat16),
            pltpu.VMEM((chunks, snp_rows, 2 * width), jnp.bfloat16),
            pltpu.SemaphoreType.DMA((2,)),
            pltpu.SemaphoreType.DMA((chunks,)),
            pltpu.SemaphoreType.DMA((4, devices, parts)),
            pltpu.SemaphoreType.DMA((devices, parts)),
            pltpu.SemaphoreType.DMA((4, devices, chunks)),
            pltpu.SemaphoreType.DMA((devices, chunks)),
        ],
        compiler_params=pltpu.CompilerParams(
            collective_id=0, has_side_effects=True, vmem_limit_bytes=EXCHANGE_LIMIT
        ),
    )(counts, snps, vectors, rider, scores)


def per_device(eig_vectors, eig_values, eig_count, snp_count, zscores, samples):
    devices = lax.axis_size("panel")
    spacing = max(1, devices // 32)
    panels = devices // spacing
    slot_index = lax.axis_index("panel")
    panel_index = slot_index // spacing
    group_index = slot_index % spacing
    blocks_here, snp_rows, panel_width = zscores.shape[1:]
    counts = lax.dynamic_slice_in_dim(eig_count, group_index * blocks_here, blocks_here)
    snps = lax.dynamic_slice_in_dim(snp_count, group_index * blocks_here, blocks_here)
    rounds = jnp.arange(ROUNDS + 1, dtype=jnp.int32)
    partners = (panel_index - rounds) % panels
    scales = samples.astype(jnp.float32).reshape(panels, panel_width)
    own_scale = lax.dynamic_index_in_dim(scales, panel_index, 0, keepdims=False)
    scale = 1.0 / jnp.sqrt(own_scale[None, :, None] * scales[partners][:, None, :])

    if spacing == 1 and panels == 2 * ROUNDS and blocks_here == panels // 2:
        raw = exchange(eig_vectors, eig_values, counts, snps, zscores)
        return raw * scale[:, None, None]
    members = [[g + spacing * i for i in range(panels)] for g in range(spacing)]
    gather = functools.partial(
        lax.all_gather, axis_name="panel", axis_index_groups=members if spacing > 1 else None
    )
    vectors = gather(eig_vectors, tiled=True)
    values = gather(eig_values, tiled=True)
    projected = project(vectors, zscores, counts, snps)
    held = gather(projected)
    weighted = (projected.astype(jnp.float32) / values.astype(jnp.float32)[:, None]).astype(
        jnp.bfloat16
    )
    return grams(weighted, held, scale, partners, counts)


def solution(mesh):
    placed = (
        P(("groups", "panel"), None),
        P(("groups", "panel")),
        P("groups"),
        P("groups"),
        P(("groups", "panel"), None, None, None),
        P("groups"),
    )
    return jax.shard_map(
        per_device,
        mesh=mesh,
        in_specs=placed,
        out_specs=P(None, ("groups", "panel"), None, None, None),
        check_vma=False,
    )
```

```python
import functools

import jax
import jax.numpy as jnp
from jax import lax
from jax.experimental import pallas as pl
from jax.experimental.pallas import tpu as pltpu
from jax.sharding import PartitionSpec as P

ROUNDS = 8
LIMIT = 56 * 1024 * 1024
EXCHANGE_LIMIT = 36 * 1024 * 1024


def place_masked(snps, scores, pair, store):
    width = scores.shape[-1]
    for side in range(2):
        block = 2 * pair + side
        rows = lax.broadcasted_iota(jnp.int32, scores.shape[-2:], 0)
        part = jnp.where(rows < snps[block], scores[side].astype(jnp.float32), 0.0)
        store[:, side * width : (side + 1) * width] = part.astype(jnp.bfloat16)


def project_rows(vectors, masked, first_count):
    both = jnp.dot(vectors, masked, preferred_element_type=jnp.float32)
    width = both.shape[1] // 2
    rows = lax.broadcasted_iota(jnp.int32, (both.shape[0], width), 0)
    return jnp.where(rows < first_count, both[:, :width], both[:, width:]).astype(jnp.bfloat16)


def project_kernel(counts, snps, vectors, scores, out, masked):
    pair = pl.program_id(0)
    place_masked(snps, scores.at[0], pair, masked)
    out[...] = project_rows(vectors[...], masked[...], counts[2 * pair])


def project(vectors, scores, counts, snps):
    row_total, depth = vectors.shape
    blocks, snp_rows, width = scores.shape[1:]
    pair_rows = 2 * row_total // blocks
    return pl.pallas_call(
        project_kernel,
        out_shape=jax.ShapeDtypeStruct((row_total, width), jnp.bfloat16),
        grid_spec=pltpu.PrefetchScalarGridSpec(
            num_scalar_prefetch=2,
            grid=(blocks // 2,),
            in_specs=[
                pl.BlockSpec((pair_rows, depth), lambda b, *_: (b, 0)),
                pl.BlockSpec((1, 2, snp_rows, width), lambda b, *_: (0, b, 0, 0)),
            ],
            out_specs=pl.BlockSpec((pair_rows, width), lambda b, *_: (b, 0)),
            scratch_shapes=[pltpu.VMEM((snp_rows, 2 * width), jnp.bfloat16)],
        ),
        compiler_params=pltpu.CompilerParams(vmem_limit_bytes=LIMIT),
    )(counts, snps, vectors, scores)


def gram_kernel(counts, slots, weighted, panels, scale, out):
    pair = pl.program_id(0)
    width = weighted.shape[1]
    left = weighted[...].astype(jnp.float32)
    rows = lax.broadcasted_iota(jnp.int32, left.shape, 0)
    first = rows < counts[2 * pair]
    left = jnp.concatenate([jnp.where(first, left, 0.0).T, jnp.where(first, 0.0, left).T], axis=0)
    left = left.astype(jnp.bfloat16)
    shape = (width, width)
    same = lax.broadcasted_iota(jnp.int32, shape, 0) == lax.broadcasted_iota(jnp.int32, shape, 1)
    for index in range(out.shape[0]):
        both = jnp.dot(left, panels[slots[index]], preferred_element_type=jnp.float32)
        for side in range(2):
            gram = both[side * width : (side + 1) * width]
            if index == 0:
                count = counts[2 * pair + side].astype(jnp.float32)
                gram = gram - jnp.where(same, count, 0.0)
            out[index, 0, side] = gram * scale[index]


def grams(weighted, panels, scale, slots, counts):
    blocks = counts.shape[0]
    rounds, width = scale.shape[:2]
    pair_rows = 2 * weighted.shape[0] // blocks
    return pl.pallas_call(
        gram_kernel,
        out_shape=jax.ShapeDtypeStruct((rounds, 1, blocks, width, width), jnp.float32),
        grid_spec=pltpu.PrefetchScalarGridSpec(
            num_scalar_prefetch=2,
            grid=(blocks // 2,),
            in_specs=[
                pl.BlockSpec((pair_rows, width), lambda b, *_: (b, 0)),
                pl.BlockSpec((panels.shape[0], pair_rows, width), lambda b, *_: (0, b, 0)),
                pl.BlockSpec(scale.shape, lambda b, *_: (0, 0, 0)),
            ],
            out_specs=pl.BlockSpec((rounds, 1, 2, width, width), lambda b, *_: (0, 0, b, 0, 0)),
        ),
        compiler_params=pltpu.CompilerParams(vmem_limit_bytes=LIMIT),
    )(counts, slots, weighted, panels, scale)


def exchange_kernel(all_counts, all_snps, own, own_values, samples, scores, out, scale, counts, snps,
                    flat_values, units, held, values, left, store, raw, masked, here, load,
                    send1, recv1, send2, recv2):
    line = lax.axis_size("panel") // 4
    me = lax.axis_index("panel")
    z = me // 4
    y = (me // 2) % 2
    k = me % 2
    piece = own.shape[0]
    pair_rows = 4 * piece
    parts = recv1.shape[1]
    part_rows = piece // (parts - 1)
    chunks = recv2.shape[1]
    top = line - 1
    inner = (z > 0) & (z < top)
    edge = (z == 0) | (z == top)
    up, down, across, beside = me + 4, me - 4, me + 2 - 4 * y, me + 1 - 2 * k
    skip = me + 8 - 16 * (z // 2)
    pending = []

    def order(plane, step):
        near = jnp.minimum(plane, top - plane)
        nearest = jnp.where(step > 2 * near, step, (near + (step + 1) // 2 * (1 - 2 * (step % 2))))
        return jnp.where(plane > top - plane, top - nearest, nearest)

    loads = []
    for step in range(line):
        pair = pl.ds(2 * order(z, step), 2)
        loads.append(
            pltpu.make_async_copy(scores.at[0, pair], raw.at[pl.ds(2 * step, 2)], load.at[step])
        )
    local = [
        pltpu.make_async_copy(own, store.at[pl.ds(me * piece, piece)], here.at[0]),
        pltpu.make_async_copy(own_values, flat_values, here.at[1]),
        pltpu.make_async_copy(all_counts, counts, here.at[2]),
        pltpu.make_async_copy(all_snps, snps, here.at[3]),
        pltpu.make_async_copy(samples, units, here.at[4]),
    ]
    for copy in local + loads:
        copy.start()

    barrier = pltpu.get_barrier_semaphore()

    def greet(target):
        pl.semaphore_signal(
            barrier, inc=1, device_id={"panel": target}, device_id_type=pl.DeviceIdType.MESH
        )

    pl.when(z < top)(functools.partial(greet, up))
    pl.when(z > 0)(functools.partial(greet, down))
    pl.when(z < 2)(functools.partial(greet, skip))
    for target in (across, beside):
        greet(target)
    for copy in local[1:]:
        copy.wait()
    spot = lax.broadcasted_iota(jnp.int32, (piece, pair_rows), 1) - lax.rem(me, 4) * piece
    hot = jnp.where(spot == lax.broadcasted_iota(jnp.int32, spot.shape, 0), 1.0, 0.0)
    ride = jnp.broadcast_to(flat_values[...].astype(jnp.float32).reshape(1, piece), (8, piece))
    ride = jnp.dot(
        ride.astype(jnp.bfloat16), hot.astype(jnp.bfloat16), preferred_element_type=jnp.float32
    )
    values[me] = ride[0:1]
    pl.semaphore_wait(barrier, 2 + jnp.where(z > 0, 1, 0) + jnp.where(z < top, 1, 0) + z // 2)

    def start(condition, copy):
        if condition is None:
            copy.start()
        else:
            pl.when(condition)(copy.start)
        pending.append((condition, copy))

    def remote(source, target, send, recv, device):
        return pltpu.make_async_remote_copy(
            src_ref=source,
            dst_ref=target,
            send_sem=send,
            recv_sem=recv,
            device_id={"panel": device},
            device_id_type=pl.DeviceIdType.MESH,
        )

    def move1(source, part, way, target, first=False):
        sems = send1.at[way, source, part], recv1.at[source, part]
        if part == parts - 1:
            return remote(values.at[source], values.at[source], *sems, target)
        rows = pl.ds(source * piece + part * part_rows, part_rows)
        origin = own.at[pl.ds(part * part_rows, part_rows)] if first else store.at[rows]
        return remote(origin, store.at[rows], *sems, target)

    def arrive1(source, part):
        move1(source, part, 0, beside).wait_recv()

    def move2(source, chunk, way, target):
        block = held.at[source, pl.ds(chunk * pair_rows, pair_rows)]
        return remote(block, block, send2.at[way, source, chunk], recv2.at[source, chunk], target)

    def arrive2(source, chunk):
        move2(source, chunk, 0, beside).wait_recv()

    def both(a, b):
        return b if a is None else a & b

    def column(step, condition=None):
        plane = order(z, step)
        source = plane * 4 + y * 2 + k
        for part in range(parts):
            if condition is None:
                arrive1(source, part)
            else:
                pl.when(condition)(functools.partial(arrive1, source, part))
            start(both(condition, (plane < z) & (z < top)), move1(source, part, 0, up))
            start(both(condition, (plane > z) & (z > 0)), move1(source, part, 1, down))
            start(condition, move1(source, part, 2, across))
            start(condition, move1(source, part, 3, beside))

    def sideways(step):
        source = order(z, step) * 4 + 2 - 2 * y + k
        for part in range(parts):
            arrive1(source, part)
            start(None, move1(source, part, 3, beside))

    def mask(step):
        loads[step].wait()
        place_masked(snps, raw.at[pl.ds(2 * step, 2)], order(z, step), masked.at[step])

    def finish(step):
        plane = order(z, step)
        for source in (plane * 4 + y * 2 + 1 - k, plane * 4 + 2 - 2 * y + 1 - k):
            for part in range(parts):
                arrive1(source, part)
        rows = pl.ds(plane * pair_rows, pair_rows)
        held[me, rows] = project_rows(store[rows], masked[step], counts[2 * plane])
        start(z < top, move2(me, plane, 0, up))
        start(k == 0, move2(me, plane, 3, beside))
        weigh(plane)

    def weigh(index):
        rows = pl.ds(index * pair_rows, pair_rows)
        row = values[4 * index] + values[4 * index + 1]
        row = row + (values[4 * index + 2] + values[4 * index + 3])
        flat = held[me, rows].astype(jnp.float32).T / row
        first = lax.broadcasted_iota(jnp.int32, flat.shape, 1) < counts[2 * index]
        both = jnp.concatenate([jnp.where(first, flat, 0.0), jnp.where(first, 0.0, flat)], axis=0)
        left[index] = both.astype(jnp.bfloat16)

    def scales():
        table = units[...].astype(jnp.float32)
        panels = lax.broadcasted_iota(jnp.int32, table.shape, 0)

        def row(panel):
            return jnp.sum(jnp.where(panels == panel, table, 0.0), axis=0, keepdims=True)

        width = table.shape[1]
        mine = jnp.broadcast_to(row(me), (width, width)).T
        for number in range(out.shape[0]):
            partner = lax.rem(me - number + 4 * line, 4 * line)
            scale[number] = 1.0 / jnp.sqrt(mine * row(partner))

    def plane_behind(lag):
        return lax.rem(z - lag + line, line)

    def own_across(step):
        start(y == 0, move2(me, order(z, step), 2, across))

    def far(step):
        start(z >= 2, move2(me, order(z, step), 1, skip))

    def relay(step, turn, condition=None):
        lag = jnp.where(z == 0, 2 - turn, 1 + turn)
        plane = plane_behind(lag)
        source = plane * 4 + y * 2 + k
        chunk = order(plane, step)
        if condition is None:
            arrive2(source, chunk)
        else:
            pl.when(condition)(functools.partial(arrive2, source, chunk))
        start(both(condition, (lag == 1) & inner), move2(source, chunk, 0, up))
        start(both(condition, (lag == 2) & (z == 1)), move2(source, chunk, 1, down))
        start(both(condition, (lag == 1) | (y == 1)), move2(source, chunk, 2, across))
        start(both(condition, (lag == 1) | (k == 1)), move2(source, chunk, 3, beside))

    cross = [plane_behind(lag + 1 - y) * 4 + (1 - y) * 2 + k for lag in range(2)]
    near = [plane_behind(lag) * 4 + y * 2 + k for lag in range(3)]
    swap = 1 - 2 * k

    def cross_over(step):
        for source in cross:
            chunk = order(source // 4, step)
            arrive2(source, chunk)
            start(None, move2(source, chunk, 3, beside))

    def gram(source, step, number, own_panel=False):
        chunk = order(source // 4, step)
        rows = pl.ds(chunk * pair_rows, pair_rows)
        both = jnp.dot(left[chunk], held[source, rows], preferred_element_type=jnp.float32)
        width = both.shape[1]
        for side in range(2):
            part = both[side * width : (side + 1) * width]
            if own_panel:
                shape = (width, width)
                across_rows = lax.broadcasted_iota(jnp.int32, shape, 0)
                same = across_rows == lax.broadcasted_iota(jnp.int32, shape, 1)
                count = counts[2 * chunk + side].astype(jnp.float32)
                part = part - jnp.where(same, count, 0.0)
            out[number, 0, 2 * chunk + side] = part

    def grams_near(step):
        for lag, source in enumerate(near):
            gram(source, step, 4 * lag, lag == 0)

    def grams_near_beside(step):
        for lag, source in enumerate(near):
            number = 4 * lag - swap

            @pl.when((number >= 0) & (number < out.shape[0]))
            def _():
                arrive2(source + swap, order(source // 4, step))
                gram(source + swap, step, number)

    def grams_cross(step):
        for lag, source in enumerate(cross):
            gram(source, step, 4 * lag + 2)

    def grams_cross_beside(step):
        for lag, source in enumerate(cross):
            arrive2(source + swap, order(source // 4, step))
            gram(source + swap, step, 4 * lag + 2 - swap)

    for part in range(parts):
        start(z < top, move1(me, part, 0, up, True))
        start(z > 0, move1(me, part, 1, down, True))
        start(None, move1(me, part, 2, across, True))
        start(None, move1(me, part, 3, beside, True))
    mask(0)
    local[0].wait()
    mask(1)
    mask(2)
    mask(3)
    scales()
    column(1)
    column(2, inner)
    sideways(0)
    finish(0)
    column(2, edge)
    column(3, inner)
    sideways(1)
    finish(1)
    far(0)
    far(1)
    relay(0, 0, inner)
    column(3, edge)
    own_across(0)
    sideways(2)
    finish(2)
    far(2)
    relay(0, 1, inner)
    relay(0, 0, edge)
    sideways(3)
    finish(3)
    far(3)
    own_across(1)
    relay(0, 1, edge)
    relay(1, 0)
    grams_near(0)
    relay(1, 1)
    cross_over(0)
    own_across(2)
    grams_near_beside(0)
    relay(2, 0)
    grams_cross(0)
    relay(2, 1)
    cross_over(1)
    own_across(3)
    grams_near(1)
    grams_cross_beside(0)
    relay(3, 0)
    grams_near_beside(1)
    grams_cross(1)
    relay(3, 1)
    cross_over(2)
    grams_cross_beside(1)
    grams_near(2)
    grams_near_beside(2)
    grams_cross(2)
    grams_near(3)
    grams_near_beside(3)
    grams_cross_beside(2)
    cross_over(3)
    grams_cross(3)
    grams_cross_beside(3)
    for condition, copy in pending:
        if condition is None:
            copy.wait_send()
        else:
            pl.when(condition)(copy.wait_send)


def exchange(vectors, values, samples, counts, snps, scores):
    devices = lax.axis_size("panel")
    piece, depth = vectors.shape
    blocks, snp_rows, width = scores.shape[1:]
    row_total = devices * piece
    pair_rows = 4 * piece
    parts = 3
    chunks = blocks // 2
    rounds = ROUNDS + 1
    hbm = pl.BlockSpec(memory_space=pltpu.HBM)
    operands = [counts, snps, vectors, values, samples.reshape(devices, width), scores]
    return pl.pallas_call(
        exchange_kernel,
        out_shape=[
            jax.ShapeDtypeStruct((rounds, 1, blocks, width, width), jnp.float32),
            jax.ShapeDtypeStruct((rounds, width, width), jnp.float32),
        ],
        in_specs=[hbm] * len(operands),
        out_specs=[pl.BlockSpec(memory_space=pltpu.VMEM)] * 2,
        scratch_shapes=[
            pltpu.SMEM((blocks,), jnp.int32),
            pltpu.SMEM((blocks,), jnp.int32),
            pltpu.VMEM((piece,), jnp.bfloat16),
            pltpu.VMEM((devices, width), jnp.bfloat16),
            pltpu.VMEM((devices, row_total, width), jnp.bfloat16),
            pltpu.VMEM((devices, 1, pair_rows), jnp.float32),
            pltpu.VMEM((chunks, 2 * width, pair_rows), jnp.bfloat16),
            pltpu.VMEM((row_total, depth), jnp.bfloat16),
            pltpu.VMEM((blocks, snp_rows, width), jnp.bfloat16),
            pltpu.VMEM((chunks, snp_rows, 2 * width), jnp.bfloat16),
            pltpu.SemaphoreType.DMA((5,)),
            pltpu.SemaphoreType.DMA((chunks,)),
            pltpu.SemaphoreType.DMA((4, devices, parts)),
            pltpu.SemaphoreType.DMA((devices, parts)),
            pltpu.SemaphoreType.DMA((4, devices, chunks)),
            pltpu.SemaphoreType.DMA((devices, chunks)),
        ],
        compiler_params=pltpu.CompilerParams(
            collective_id=0, has_side_effects=True, vmem_limit_bytes=EXCHANGE_LIMIT
        ),
    )(*[pltpu.with_memory_space_constraint(operand, pltpu.HBM) for operand in operands])


def per_device(eig_vectors, eig_values, eig_count, snp_count, zscores, samples):
    devices = lax.axis_size("panel")
    spacing = max(1, devices // 32)
    panels = devices // spacing
    slot_index = lax.axis_index("panel")
    panel_index = slot_index // spacing
    group_index = slot_index % spacing
    blocks_here, snp_rows, panel_width = zscores.shape[1:]
    if spacing == 1 and panels == 2 * ROUNDS and blocks_here == panels // 2:
        raw, scale = exchange(eig_vectors, eig_values, samples, eig_count, snp_count, zscores)
        return raw * scale[:, None, None]
    counts = lax.dynamic_slice_in_dim(eig_count, group_index * blocks_here, blocks_here)
    snps = lax.dynamic_slice_in_dim(snp_count, group_index * blocks_here, blocks_here)
    rounds = jnp.arange(ROUNDS + 1, dtype=jnp.int32)
    partners = (panel_index - rounds) % panels
    scales = samples.astype(jnp.float32).reshape(panels, panel_width)
    own_scale = lax.dynamic_index_in_dim(scales, panel_index, 0, keepdims=False)
    scale = 1.0 / jnp.sqrt(own_scale[None, :, None] * scales[partners][:, None, :])
    members = [[g + spacing * i for i in range(panels)] for g in range(spacing)]
    gather = functools.partial(
        lax.all_gather, axis_name="panel", axis_index_groups=members if spacing > 1 else None
    )
    vectors = gather(eig_vectors, tiled=True)
    values = gather(eig_values, tiled=True)
    projected = project(vectors, zscores, counts, snps)
    held = gather(projected)
    weighted = (projected.astype(jnp.float32) / values.astype(jnp.float32)[:, None]).astype(
        jnp.bfloat16
    )
    return grams(weighted, held, scale, partners, counts)


def solution(mesh):
    placed = (
        P(("groups", "panel"), None),
        P(("groups", "panel")),
        P("groups"),
        P("groups"),
        P(("groups", "panel"), None, None, None),
        P("groups"),
    )
    return jax.shard_map(
        per_device,
        mesh=mesh,
        in_specs=placed,
        out_specs=P(None, ("groups", "panel"), None, None, None),
        check_vma=False,
    )
```

```python
import functools

import jax
import jax.numpy as jnp
from jax import lax
from jax.experimental import pallas as pl
from jax.experimental.pallas import tpu as pltpu
from jax.sharding import PartitionSpec as P

ROUNDS = 8
LIMIT = 56 * 1024 * 1024
EXCHANGE_LIMIT = 36 * 1024 * 1024


def place_masked(snps, scores, pair, store):
    width = scores.shape[-1]
    for side in range(2):
        block = 2 * pair + side
        rows = lax.broadcasted_iota(jnp.int32, scores.shape[-2:], 0)
        part = jnp.where(rows < snps[block], scores[side].astype(jnp.float32), 0.0)
        store[:, side * width : (side + 1) * width] = part.astype(jnp.bfloat16)


def project_rows(vectors, masked, first_count):
    both = jnp.dot(vectors, masked, preferred_element_type=jnp.float32)
    width = both.shape[1] // 2
    rows = lax.broadcasted_iota(jnp.int32, (both.shape[0], width), 0)
    return jnp.where(rows < first_count, both[:, :width], both[:, width:]).astype(jnp.bfloat16)


def project_kernel(counts, snps, vectors, scores, out, masked):
    pair = pl.program_id(0)
    place_masked(snps, scores.at[0], pair, masked)
    out[...] = project_rows(vectors[...], masked[...], counts[2 * pair])


def project(vectors, scores, counts, snps):
    row_total, depth = vectors.shape
    blocks, snp_rows, width = scores.shape[1:]
    pair_rows = 2 * row_total // blocks
    return pl.pallas_call(
        project_kernel,
        out_shape=jax.ShapeDtypeStruct((row_total, width), jnp.bfloat16),
        grid_spec=pltpu.PrefetchScalarGridSpec(
            num_scalar_prefetch=2,
            grid=(blocks // 2,),
            in_specs=[
                pl.BlockSpec((pair_rows, depth), lambda b, *_: (b, 0)),
                pl.BlockSpec((1, 2, snp_rows, width), lambda b, *_: (0, b, 0, 0)),
            ],
            out_specs=pl.BlockSpec((pair_rows, width), lambda b, *_: (b, 0)),
            scratch_shapes=[pltpu.VMEM((snp_rows, 2 * width), jnp.bfloat16)],
        ),
        compiler_params=pltpu.CompilerParams(vmem_limit_bytes=LIMIT),
    )(counts, snps, vectors, scores)


def gram_kernel(counts, slots, weighted, panels, scale, out):
    pair = pl.program_id(0)
    width = weighted.shape[1]
    left = weighted[...].astype(jnp.float32)
    rows = lax.broadcasted_iota(jnp.int32, left.shape, 0)
    first = rows < counts[2 * pair]
    left = jnp.concatenate([jnp.where(first, left, 0.0).T, jnp.where(first, 0.0, left).T], axis=0)
    left = left.astype(jnp.bfloat16)
    shape = (width, width)
    same = lax.broadcasted_iota(jnp.int32, shape, 0) == lax.broadcasted_iota(jnp.int32, shape, 1)
    for index in range(out.shape[0]):
        both = jnp.dot(left, panels[slots[index]], preferred_element_type=jnp.float32)
        for side in range(2):
            gram = both[side * width : (side + 1) * width]
            if index == 0:
                count = counts[2 * pair + side].astype(jnp.float32)
                gram = gram - jnp.where(same, count, 0.0)
            out[index, 0, side] = gram * scale[index]


def grams(weighted, panels, scale, slots, counts):
    blocks = counts.shape[0]
    rounds, width = scale.shape[:2]
    pair_rows = 2 * weighted.shape[0] // blocks
    return pl.pallas_call(
        gram_kernel,
        out_shape=jax.ShapeDtypeStruct((rounds, 1, blocks, width, width), jnp.float32),
        grid_spec=pltpu.PrefetchScalarGridSpec(
            num_scalar_prefetch=2,
            grid=(blocks // 2,),
            in_specs=[
                pl.BlockSpec((pair_rows, width), lambda b, *_: (b, 0)),
                pl.BlockSpec((panels.shape[0], pair_rows, width), lambda b, *_: (0, b, 0)),
                pl.BlockSpec(scale.shape, lambda b, *_: (0, 0, 0)),
            ],
            out_specs=pl.BlockSpec((rounds, 1, 2, width, width), lambda b, *_: (0, 0, b, 0, 0)),
        ),
        compiler_params=pltpu.CompilerParams(vmem_limit_bytes=LIMIT),
    )(counts, slots, weighted, panels, scale)


def exchange_kernel(all_counts, all_snps, own, own_values, samples, scores, out, scale, counts, snps,
                    flat_values, units, held, values, left, store, raw, masked, here, load,
                    sent, recv1, recv2):
    line = lax.axis_size("panel") // 4
    me = lax.axis_index("panel")
    z = me // 4
    y = (me // 2) % 2
    k = me % 2
    piece = own.shape[0]
    pair_rows = 4 * piece
    parts = recv1.shape[1]
    part_rows = piece // (parts - 1)
    chunks = recv2.shape[1]
    top = line - 1
    inner = (z > 0) & (z < top)
    edge = (z == 0) | (z == top)
    up, down, across, beside = me + 4, me - 4, me + 2 - 4 * y, me + 1 - 2 * k
    skip = me + 8 - 16 * (z // 2)
    pending = []

    def order(plane, step):
        near = jnp.minimum(plane, top - plane)
        nearest = jnp.where(step > 2 * near, step, (near + (step + 1) // 2 * (1 - 2 * (step % 2))))
        return jnp.where(plane > top - plane, top - nearest, nearest)

    loads = []
    for step in range(line):
        pair = pl.ds(2 * order(z, step), 2)
        loads.append(
            pltpu.make_async_copy(scores.at[0, pair], raw.at[pl.ds(2 * step, 2)], load.at[step])
        )
    local = [
        pltpu.make_async_copy(own, store.at[pl.ds(me * piece, piece)], here.at[0]),
        pltpu.make_async_copy(own_values, flat_values, here.at[1]),
        pltpu.make_async_copy(all_counts, counts, here.at[2]),
        pltpu.make_async_copy(all_snps, snps, here.at[3]),
        pltpu.make_async_copy(samples, units, here.at[4]),
    ]
    for copy in local + loads:
        copy.start()

    barrier = pltpu.get_barrier_semaphore()

    def greet(target):
        pl.semaphore_signal(
            barrier, inc=1, device_id={"panel": target}, device_id_type=pl.DeviceIdType.MESH
        )

    pl.when(z < top)(functools.partial(greet, up))
    pl.when(z > 0)(functools.partial(greet, down))
    pl.when(z < 2)(functools.partial(greet, skip))
    for target in (across, beside):
        greet(target)
    for copy in local[1:]:
        copy.wait()
    spot = lax.broadcasted_iota(jnp.int32, (piece, pair_rows), 1) - lax.rem(me, 4) * piece
    hot = jnp.where(spot == lax.broadcasted_iota(jnp.int32, spot.shape, 0), 1.0, 0.0)
    ride = jnp.broadcast_to(flat_values[...].astype(jnp.float32).reshape(1, piece), (8, piece))
    ride = jnp.dot(
        ride.astype(jnp.bfloat16), hot.astype(jnp.bfloat16), preferred_element_type=jnp.float32
    )
    values[me] = ride[0:1]
    pl.semaphore_wait(barrier, 2 + jnp.where(z > 0, 1, 0) + jnp.where(z < top, 1, 0) + z // 2)

    def start(condition, copy):
        if condition is None:
            copy.start()
        else:
            pl.when(condition)(copy.start)
        pending.append((condition, copy))

    def remote(source, target, send, recv, device):
        return pltpu.make_async_remote_copy(
            src_ref=source,
            dst_ref=target,
            send_sem=send,
            recv_sem=recv,
            device_id={"panel": device},
            device_id_type=pl.DeviceIdType.MESH,
        )

    def move1(source, part, way, target, first=False):
        sems = sent.at[0], recv1.at[source, part]
        if part == parts - 1:
            return remote(values.at[source], values.at[source], *sems, target)
        rows = pl.ds(source * piece + part * part_rows, part_rows)
        origin = own.at[pl.ds(part * part_rows, part_rows)] if first else store.at[rows]
        return remote(origin, store.at[rows], *sems, target)

    def arrive1(source, part):
        move1(source, part, 0, beside).wait_recv()

    def move2(source, chunk, way, target):
        block = held.at[source, pl.ds(chunk * pair_rows, pair_rows)]
        return remote(block, block, sent.at[1], recv2.at[source, chunk], target)

    def arrive2(source, chunk):
        move2(source, chunk, 0, beside).wait_recv()

    def both(a, b):
        return b if a is None else a & b

    def column(step, condition=None):
        plane = order(z, step)
        source = plane * 4 + y * 2 + k
        for part in range(parts):
            if condition is None:
                arrive1(source, part)
            else:
                pl.when(condition)(functools.partial(arrive1, source, part))
            start(both(condition, (plane < z) & (z < top)), move1(source, part, 0, up))
            start(both(condition, (plane > z) & (z > 0)), move1(source, part, 1, down))
            start(condition, move1(source, part, 2, across))
            start(condition, move1(source, part, 3, beside))

    def sideways(step):
        source = order(z, step) * 4 + 2 - 2 * y + k
        for part in range(parts):
            arrive1(source, part)
            start(None, move1(source, part, 3, beside))

    def mask(step):
        loads[step].wait()
        place_masked(snps, raw.at[pl.ds(2 * step, 2)], order(z, step), masked.at[step])

    def finish(step):
        plane = order(z, step)
        for source in (plane * 4 + y * 2 + 1 - k, plane * 4 + 2 - 2 * y + 1 - k):
            for part in range(parts):
                arrive1(source, part)
        rows = pl.ds(plane * pair_rows, pair_rows)
        held[me, rows] = project_rows(store[rows], masked[step], counts[2 * plane])
        start(z < top, move2(me, plane, 0, up))
        start(k == 0, move2(me, plane, 3, beside))
        weigh(plane)

    def weigh(index):
        rows = pl.ds(index * pair_rows, pair_rows)
        row = values[4 * index] + values[4 * index + 1]
        row = row + (values[4 * index + 2] + values[4 * index + 3])
        flat = held[me, rows].astype(jnp.float32).T / row
        first = lax.broadcasted_iota(jnp.int32, flat.shape, 1) < counts[2 * index]
        both = jnp.concatenate([jnp.where(first, flat, 0.0), jnp.where(first, 0.0, flat)], axis=0)
        left[index] = both.astype(jnp.bfloat16)

    def scales():
        table = units[...].astype(jnp.float32)
        panels = lax.broadcasted_iota(jnp.int32, table.shape, 0)

        def row(panel):
            return jnp.sum(jnp.where(panels == panel, table, 0.0), axis=0, keepdims=True)

        width = table.shape[1]
        mine = jnp.broadcast_to(row(me), (width, width)).T
        for number in range(out.shape[0]):
            partner = lax.rem(me - number + 4 * line, 4 * line)
            scale[number] = 1.0 / jnp.sqrt(mine * row(partner))

    def plane_behind(lag):
        return lax.rem(z - lag + line, line)

    def own_across(step):
        start(y == 0, move2(me, order(z, step), 2, across))

    def far(step):
        start(z >= 2, move2(me, order(z, step), 1, skip))

    def relay(step, turn, condition=None):
        lag = jnp.where(z == 0, 2 - turn, 1 + turn)
        plane = plane_behind(lag)
        source = plane * 4 + y * 2 + k
        chunk = order(plane, step)
        if condition is None:
            arrive2(source, chunk)
        else:
            pl.when(condition)(functools.partial(arrive2, source, chunk))
        start(both(condition, (lag == 1) & inner), move2(source, chunk, 0, up))
        start(both(condition, (lag == 2) & (z == 1)), move2(source, chunk, 1, down))
        start(both(condition, (lag == 1) | (y == 1)), move2(source, chunk, 2, across))
        start(both(condition, (lag == 1) | (k == 1)), move2(source, chunk, 3, beside))

    cross = [plane_behind(lag + 1 - y) * 4 + (1 - y) * 2 + k for lag in range(2)]
    near = [plane_behind(lag) * 4 + y * 2 + k for lag in range(3)]
    swap = 1 - 2 * k

    def cross_over(step):
        for source in cross:
            chunk = order(source // 4, step)
            arrive2(source, chunk)
            start(None, move2(source, chunk, 3, beside))

    def gram(source, step, number, own_panel=False):
        chunk = order(source // 4, step)
        rows = pl.ds(chunk * pair_rows, pair_rows)
        both = jnp.dot(left[chunk], held[source, rows], preferred_element_type=jnp.float32)
        width = both.shape[1]
        for side in range(2):
            part = both[side * width : (side + 1) * width]
            if own_panel:
                shape = (width, width)
                across_rows = lax.broadcasted_iota(jnp.int32, shape, 0)
                same = across_rows == lax.broadcasted_iota(jnp.int32, shape, 1)
                count = counts[2 * chunk + side].astype(jnp.float32)
                part = part - jnp.where(same, count, 0.0)
            out[number, 0, 2 * chunk + side] = part

    def grams_near(step):
        for lag, source in enumerate(near):
            gram(source, step, 4 * lag, lag == 0)

    def grams_near_beside(step):
        for lag, source in enumerate(near):
            number = 4 * lag - swap

            @pl.when((number >= 0) & (number < out.shape[0]))
            def _():
                arrive2(source + swap, order(source // 4, step))
                gram(source + swap, step, number)

    def grams_cross(step):
        for lag, source in enumerate(cross):
            gram(source, step, 4 * lag + 2)

    def grams_cross_beside(step):
        for lag, source in enumerate(cross):
            arrive2(source + swap, order(source // 4, step))
            gram(source + swap, step, 4 * lag + 2 - swap)

    for part in range(parts):
        start(z < top, move1(me, part, 0, up, True))
        start(z > 0, move1(me, part, 1, down, True))
        start(None, move1(me, part, 2, across, True))
        start(None, move1(me, part, 3, beside, True))
    mask(0)
    local[0].wait()
    mask(1)
    mask(2)
    mask(3)
    scales()
    column(1)
    column(2, inner)
    sideways(0)
    finish(0)
    column(2, edge)
    column(3, inner)
    sideways(1)
    finish(1)
    far(0)
    far(1)
    relay(0, 0, inner)
    column(3, edge)
    own_across(0)
    sideways(2)
    finish(2)
    far(2)
    relay(0, 1, inner)
    relay(0, 0, edge)
    sideways(3)
    finish(3)
    far(3)
    own_across(1)
    relay(0, 1, edge)
    relay(1, 0)
    grams_near(0)
    relay(1, 1)
    cross_over(0)
    own_across(2)
    grams_near_beside(0)
    relay(2, 0)
    grams_cross(0)
    relay(2, 1)
    cross_over(1)
    own_across(3)
    grams_near(1)
    grams_cross_beside(0)
    relay(3, 0)
    grams_near_beside(1)
    grams_cross(1)
    relay(3, 1)
    cross_over(2)
    grams_cross_beside(1)
    grams_near(2)
    grams_near_beside(2)
    grams_cross(2)
    grams_near(3)
    grams_near_beside(3)
    grams_cross_beside(2)
    cross_over(3)
    grams_cross(3)
    grams_cross_beside(3)
    for condition, copy in pending:
        if condition is None:
            copy.wait_send()
        else:
            pl.when(condition)(copy.wait_send)


def exchange(vectors, values, samples, counts, snps, scores):
    devices = lax.axis_size("panel")
    piece, depth = vectors.shape
    blocks, snp_rows, width = scores.shape[1:]
    row_total = devices * piece
    pair_rows = 4 * piece
    parts = 3
    chunks = blocks // 2
    rounds = ROUNDS + 1
    hbm = pl.BlockSpec(memory_space=pltpu.HBM)
    operands = [counts, snps, vectors, values, samples.reshape(devices, width), scores]
    return pl.pallas_call(
        exchange_kernel,
        out_shape=[
            jax.ShapeDtypeStruct((rounds, 1, blocks, width, width), jnp.float32),
            jax.ShapeDtypeStruct((rounds, width, width), jnp.float32),
        ],
        in_specs=[hbm] * len(operands),
        out_specs=[pl.BlockSpec(memory_space=pltpu.VMEM)] * 2,
        scratch_shapes=[
            pltpu.SMEM((blocks,), jnp.int32),
            pltpu.SMEM((blocks,), jnp.int32),
            pltpu.VMEM((piece,), jnp.bfloat16),
            pltpu.VMEM((devices, width), jnp.bfloat16),
            pltpu.VMEM((devices, row_total, width), jnp.bfloat16),
            pltpu.VMEM((devices, 1, pair_rows), jnp.float32),
            pltpu.VMEM((chunks, 2 * width, pair_rows), jnp.bfloat16),
            pltpu.VMEM((row_total, depth), jnp.bfloat16),
            pltpu.VMEM((blocks, snp_rows, width), jnp.bfloat16),
            pltpu.VMEM((chunks, snp_rows, 2 * width), jnp.bfloat16),
            pltpu.SemaphoreType.DMA((5,)),
            pltpu.SemaphoreType.DMA((chunks,)),
            pltpu.SemaphoreType.DMA((2,)),
            pltpu.SemaphoreType.DMA((devices, parts)),
            pltpu.SemaphoreType.DMA((devices, chunks)),
        ],
        compiler_params=pltpu.CompilerParams(
            collective_id=0, has_side_effects=True, vmem_limit_bytes=EXCHANGE_LIMIT
        ),
    )(*[pltpu.with_memory_space_constraint(operand, pltpu.HBM) for operand in operands])


def per_device(eig_vectors, eig_values, eig_count, snp_count, zscores, samples):
    devices = lax.axis_size("panel")
    spacing = max(1, devices // 32)
    panels = devices // spacing
    slot_index = lax.axis_index("panel")
    panel_index = slot_index // spacing
    group_index = slot_index % spacing
    blocks_here, snp_rows, panel_width = zscores.shape[1:]
    if spacing == 1 and panels == 2 * ROUNDS and blocks_here == panels // 2:
        raw, scale = exchange(eig_vectors, eig_values, samples, eig_count, snp_count, zscores)
        return raw * scale[:, None, None]
    counts = lax.dynamic_slice_in_dim(eig_count, group_index * blocks_here, blocks_here)
    snps = lax.dynamic_slice_in_dim(snp_count, group_index * blocks_here, blocks_here)
    rounds = jnp.arange(ROUNDS + 1, dtype=jnp.int32)
    partners = (panel_index - rounds) % panels
    scales = samples.astype(jnp.float32).reshape(panels, panel_width)
    own_scale = lax.dynamic_index_in_dim(scales, panel_index, 0, keepdims=False)
    scale = 1.0 / jnp.sqrt(own_scale[None, :, None] * scales[partners][:, None, :])
    members = [[g + spacing * i for i in range(panels)] for g in range(spacing)]
    gather = functools.partial(
        lax.all_gather, axis_name="panel", axis_index_groups=members if spacing > 1 else None
    )
    vectors = gather(eig_vectors, tiled=True)
    values = gather(eig_values, tiled=True)
    projected = project(vectors, zscores, counts, snps)
    held = gather(projected)
    weighted = (projected.astype(jnp.float32) / values.astype(jnp.float32)[:, None]).astype(
        jnp.bfloat16
    )
    return grams(weighted, held, scale, partners, counts)


def solution(mesh):
    placed = (
        P(("groups", "panel"), None),
        P(("groups", "panel")),
        P("groups"),
        P("groups"),
        P(("groups", "panel"), None, None, None),
        P("groups"),
    )
    return jax.shard_map(
        per_device,
        mesh=mesh,
        in_specs=placed,
        out_specs=P(None, ("groups", "panel"), None, None, None),
        check_vma=False,
    )
```

```python
import functools

import jax
import jax.numpy as jnp
from jax import lax
from jax.experimental import pallas as pl
from jax.experimental.pallas import tpu as pltpu
from jax.sharding import PartitionSpec as P

ROUNDS = 8
LIMIT = 56 * 1024 * 1024
EXCHANGE_LIMIT = 36 * 1024 * 1024


def place_masked(snps, scores, pair, store):
    width = scores.shape[-1]
    for side in range(2):
        block = 2 * pair + side
        rows = lax.broadcasted_iota(jnp.int32, scores.shape[-2:], 0)
        part = jnp.where(rows < snps[block], scores[side].astype(jnp.float32), 0.0)
        store[:, side * width : (side + 1) * width] = part.astype(jnp.bfloat16)


def project_rows(vectors, masked, first_count):
    both = jnp.dot(vectors, masked, preferred_element_type=jnp.float32)
    width = both.shape[1] // 2
    rows = lax.broadcasted_iota(jnp.int32, (both.shape[0], width), 0)
    return jnp.where(rows < first_count, both[:, :width], both[:, width:]).astype(jnp.bfloat16)


def project_kernel(counts, snps, vectors, scores, out, masked):
    pair = pl.program_id(0)
    place_masked(snps, scores.at[0], pair, masked)
    out[...] = project_rows(vectors[...], masked[...], counts[2 * pair])


def project(vectors, scores, counts, snps):
    row_total, depth = vectors.shape
    blocks, snp_rows, width = scores.shape[1:]
    pair_rows = 2 * row_total // blocks
    return pl.pallas_call(
        project_kernel,
        out_shape=jax.ShapeDtypeStruct((row_total, width), jnp.bfloat16),
        grid_spec=pltpu.PrefetchScalarGridSpec(
            num_scalar_prefetch=2,
            grid=(blocks // 2,),
            in_specs=[
                pl.BlockSpec((pair_rows, depth), lambda b, *_: (b, 0)),
                pl.BlockSpec((1, 2, snp_rows, width), lambda b, *_: (0, b, 0, 0)),
            ],
            out_specs=pl.BlockSpec((pair_rows, width), lambda b, *_: (b, 0)),
            scratch_shapes=[pltpu.VMEM((snp_rows, 2 * width), jnp.bfloat16)],
        ),
        compiler_params=pltpu.CompilerParams(vmem_limit_bytes=LIMIT),
    )(counts, snps, vectors, scores)


def gram_kernel(counts, slots, weighted, panels, scale, out):
    pair = pl.program_id(0)
    width = weighted.shape[1]
    left = weighted[...].astype(jnp.float32)
    rows = lax.broadcasted_iota(jnp.int32, left.shape, 0)
    first = rows < counts[2 * pair]
    left = jnp.concatenate([jnp.where(first, left, 0.0).T, jnp.where(first, 0.0, left).T], axis=0)
    left = left.astype(jnp.bfloat16)
    shape = (width, width)
    same = lax.broadcasted_iota(jnp.int32, shape, 0) == lax.broadcasted_iota(jnp.int32, shape, 1)
    for index in range(out.shape[0]):
        both = jnp.dot(left, panels[slots[index]], preferred_element_type=jnp.float32)
        for side in range(2):
            gram = both[side * width : (side + 1) * width]
            if index == 0:
                count = counts[2 * pair + side].astype(jnp.float32)
                gram = gram - jnp.where(same, count, 0.0)
            out[index, 0, side] = gram * scale[index]


def grams(weighted, panels, scale, slots, counts):
    blocks = counts.shape[0]
    rounds, width = scale.shape[:2]
    pair_rows = 2 * weighted.shape[0] // blocks
    return pl.pallas_call(
        gram_kernel,
        out_shape=jax.ShapeDtypeStruct((rounds, 1, blocks, width, width), jnp.float32),
        grid_spec=pltpu.PrefetchScalarGridSpec(
            num_scalar_prefetch=2,
            grid=(blocks // 2,),
            in_specs=[
                pl.BlockSpec((pair_rows, width), lambda b, *_: (b, 0)),
                pl.BlockSpec((panels.shape[0], pair_rows, width), lambda b, *_: (0, b, 0)),
                pl.BlockSpec(scale.shape, lambda b, *_: (0, 0, 0)),
            ],
            out_specs=pl.BlockSpec((rounds, 1, 2, width, width), lambda b, *_: (0, 0, b, 0, 0)),
        ),
        compiler_params=pltpu.CompilerParams(vmem_limit_bytes=LIMIT),
    )(counts, slots, weighted, panels, scale)


def exchange_kernel(all_counts, all_snps, own, own_values, samples, scores, out, scale, counts, snps,
                    flat_values, units, held, values, left, store, raw, masked, here, load, shipped,
                    sent, recv1, recv2):
    line = lax.axis_size("panel") // 4
    me = lax.axis_index("panel")
    z = me // 4
    y = (me // 2) % 2
    k = me % 2
    piece = own.shape[0]
    pair_rows = 4 * piece
    parts = recv1.shape[1]
    part_rows = piece // (parts - 1)
    chunks = recv2.shape[1]
    top = line - 1
    inner = (z > 0) & (z < top)
    edge = (z == 0) | (z == top)
    up, down, across, beside = me + 4, me - 4, me + 2 - 4 * y, me + 1 - 2 * k
    inward = jnp.where(z == 0, up, down)
    outward = jnp.where(z == 1, down, up)
    pending = []

    def order(plane, step):
        near = jnp.minimum(plane, top - plane)
        nearest = jnp.where(step > 2 * near, step, (near + (step + 1) // 2 * (1 - 2 * (step % 2))))
        return jnp.where(plane > top - plane, top - nearest, nearest)

    loads = []
    for step in range(line):
        pair = pl.ds(2 * order(z, step), 2)
        loads.append(
            pltpu.make_async_copy(scores.at[0, pair], raw.at[pl.ds(2 * step, 2)], load.at[step])
        )
    local = [
        pltpu.make_async_copy(own, store.at[pl.ds(me * piece, piece)], here.at[0]),
        pltpu.make_async_copy(own_values, flat_values, here.at[1]),
        pltpu.make_async_copy(all_counts, counts, here.at[2]),
        pltpu.make_async_copy(all_snps, snps, here.at[3]),
        pltpu.make_async_copy(samples, units, here.at[4]),
    ]
    for copy in local + loads:
        copy.start()

    barrier = pltpu.get_barrier_semaphore()

    def greet(target):
        pl.semaphore_signal(
            barrier, inc=1, device_id={"panel": target}, device_id_type=pl.DeviceIdType.MESH
        )

    pl.when(z < top)(functools.partial(greet, up))
    pl.when(z > 0)(functools.partial(greet, down))
    for target in (across, beside):
        greet(target)
    for copy in local[1:]:
        copy.wait()
    spot = lax.broadcasted_iota(jnp.int32, (piece, pair_rows), 1) - lax.rem(me, 4) * piece
    hot = jnp.where(spot == lax.broadcasted_iota(jnp.int32, spot.shape, 0), 1.0, 0.0)
    ride = jnp.broadcast_to(flat_values[...].astype(jnp.float32).reshape(1, piece), (8, piece))
    ride = jnp.dot(
        ride.astype(jnp.bfloat16), hot.astype(jnp.bfloat16), preferred_element_type=jnp.float32
    )
    values[me] = ride[0:1]
    pl.semaphore_wait(barrier, jnp.where(inner, 4, 3))

    def start(condition, copy):
        if condition is None:
            copy.start()
        else:
            pl.when(condition)(copy.start)
        pending.append((condition, copy))

    def remote(source, target, send, recv, device):
        return pltpu.make_async_remote_copy(
            src_ref=source,
            dst_ref=target,
            send_sem=send,
            recv_sem=recv,
            device_id={"panel": device},
            device_id_type=pl.DeviceIdType.MESH,
        )

    def move1(source, part, way, target, first=False):
        sems = sent.at[0], recv1.at[source, part]
        if part == parts - 1:
            return remote(values.at[source], values.at[source], *sems, target)
        rows = pl.ds(source * piece + part * part_rows, part_rows)
        origin = own.at[pl.ds(part * part_rows, part_rows)] if first else store.at[rows]
        return remote(origin, store.at[rows], *sems, target)

    def arrive1(source, part):
        move1(source, part, 0, beside).wait_recv()

    def move2(source, chunk, way, target):
        block = held.at[source, pl.ds(chunk * pair_rows, pair_rows)]
        return remote(block, block, sent.at[1], recv2.at[source, chunk], target)

    def arrive2(source, chunk):
        move2(source, chunk, 0, beside).wait_recv()

    def both(a, b):
        return b if a is None else a & b

    def column(step, condition, some=None):
        plane = order(z, step)
        source = plane * 4 + y * 2 + k
        for part in range(parts) if some is None else some:
            wait(condition, arrive1, source, part)
            if step < top or part == parts - 1:
                start(condition & (plane < z) & (z < top), move1(source, part, 0, up))
                held_back = (z == 2) if step == 1 and part > 0 else (z < 0)
                start(condition & (plane > z) & (z > 0) & ~held_back, move1(source, part, 1, down))
            if step == 1:
                start(condition & edge, move1(source, part, 2, across))
            else:
                start(condition, move1(source, part, 2, across))
            start(condition, move1(source, part, 3, beside))

    def column_rest():
        for part in range(1, parts):
            start(z == 2, move1(me + 4, part, 1, down))

    def passing(step, condition):
        source, chunk = me + 4, order(z + 1, step)
        wait(condition, arrive2, source, chunk)
        start(condition, move2(source, chunk, 1, down))

    def sideways(step, condition=None, some=None):
        source = order(z, step) * 4 + 2 - 2 * y + k
        for part in range(parts) if some is None else some:
            wait(condition, arrive1, source, part)
            start(condition, move1(source, part, 3, beside))
            if step == 0:
                start(both(condition, edge), move1(source, part, 0, inward))

    def mask(step):
        loads[step].wait()
        place_masked(snps, raw.at[pl.ds(2 * step, 2)], order(z, step), masked.at[step])

    def wait(condition, arrive, *where):
        if condition is None:
            arrive(*where)
        else:
            pl.when(condition)(functools.partial(arrive, *where))

    def beside_pieces(step, condition, some):
        plane = order(z, step)
        for source in (plane * 4 + y * 2 + 1 - k, plane * 4 + 2 - 2 * y + 1 - k):
            for part in some:
                wait(condition, arrive1, source, part)

    def compute(step):
        plane = order(z, step)
        rows = pl.ds(plane * pair_rows, pair_rows)
        held[me, rows] = project_rows(store[rows], masked[step], counts[2 * plane])

    def finish(step, condition=None):
        plane = order(z, step)
        beside_pieces(step, condition, range(parts))
        wait(condition, compute, step)
        start(both(condition, z < top), move2(me, plane, 0, up))
        start((z == 2) if step == top else (z >= 2), move2(me, plane, 1, down))
        start(both(condition, k == 0), move2(me, plane, 3, beside))
        wait(condition, weigh, plane)

    def ship(half):
        block = 2 * order(z, top) + half
        return remote(
            scores.at[0, pl.ds(block, 1)],
            raw.at[pl.ds(2 * line + half, 1)],
            sent.at[2],
            shipped.at[half],
            inward,
        )

    def compute_outside():
        plane = order(z, top)
        for half in range(2):
            ship(half).wait_recv()
        place_masked(snps, raw.at[pl.ds(2 * line, 2)], plane, masked.at[line])
        rows = pl.ds(plane * pair_rows, pair_rows)
        held[outward, rows] = project_rows(store[rows], masked[line], counts[2 * plane])

    def outside():
        plane = order(z, top)
        pl.when(inner)(compute_outside)
        start(inner, move2(outward, plane, 0, up))
        start(inner & ~late_return, move2(outward, plane, 1, down))
        start(z == 1, move2(outward, plane, 2, across))
        start(z == 1, move2(outward, plane, 3, beside))

    late_return = (z == 1) & (y == 1)

    def outside_rest():
        start(late_return, move2(outward, order(z, top), 1, down))

    def returned(condition):
        plane = order(z, top)
        beside_pieces(top, condition, [parts - 1])
        wait(condition, arrive2, me, plane)
        start(condition & (k == 0), move2(me, plane, 3, beside))
        start(condition & (y == 0), move2(me, plane, 2, across))
        wait(condition, weigh, plane)

    def weigh(index):
        rows = pl.ds(index * pair_rows, pair_rows)
        row = values[4 * index] + values[4 * index + 1]
        row = row + (values[4 * index + 2] + values[4 * index + 3])
        flat = held[me, rows].astype(jnp.float32).T / row
        first = lax.broadcasted_iota(jnp.int32, flat.shape, 1) < counts[2 * index]
        both = jnp.concatenate([jnp.where(first, flat, 0.0), jnp.where(first, 0.0, flat)], axis=0)
        left[index] = both.astype(jnp.bfloat16)

    def scales():
        table = units[...].astype(jnp.float32)
        panels = lax.broadcasted_iota(jnp.int32, table.shape, 0)

        def row(panel):
            return jnp.sum(jnp.where(panels == panel, table, 0.0), axis=0, keepdims=True)

        width = table.shape[1]
        mine = jnp.broadcast_to(row(me), (width, width)).T
        for number in range(out.shape[0]):
            partner = lax.rem(me - number + 4 * line, 4 * line)
            scale[number] = 1.0 / jnp.sqrt(mine * row(partner))

    def plane_behind(lag):
        return lax.rem(z - lag + line, line)

    def own_across(step, condition=None):
        start(both(condition, y == 0), move2(me, order(z, step), 2, across))

    def relay(step, turn, condition=None):
        lag = jnp.where(z == 0, 2 - turn, 1 + turn)
        plane = plane_behind(lag)
        source = plane * 4 + y * 2 + k
        chunk = order(plane, step)
        wait(condition, arrive2, source, chunk)
        start(both(condition, (lag == 1) & inner), move2(source, chunk, 0, up))
        start(both(condition, (lag == 2) & (z == 1)), move2(source, chunk, 1, down))
        start(both(condition, (lag == 1) | (y == 1)), move2(source, chunk, 2, across))
        start(both(condition, (lag == 1) | (k == 1)), move2(source, chunk, 3, beside))

    cross = [plane_behind(lag + 1 - y) * 4 + (1 - y) * 2 + k for lag in range(2)]
    swap = 1 - 2 * k

    def cross_over(step):
        for source in cross:
            chunk = order(source // 4, step)
            arrive2(source, chunk)
            start(None, move2(source, chunk, 3, beside))

    def turn_of(source, place):
        plane = source // 4
        late = sum(jnp.where(order(plane, step) == order(z, top), step, 0) for step in range(line))
        if place == 2:
            step = late
        else:
            rank = min(place, 2)
            step = rank + jnp.where(rank >= late, 1, 0)
        return order(plane, jnp.where(edge, step, place))

    def gram(source, step, number, own_panel=False):
        chunk = turn_of(source, step)
        rows = pl.ds(chunk * pair_rows, pair_rows)
        both = jnp.dot(left[chunk], held[source, rows], preferred_element_type=jnp.float32)
        width = both.shape[1]
        for side in range(2):
            part = both[side * width : (side + 1) * width]
            if own_panel:
                shape = (width, width)
                across_rows = lax.broadcasted_iota(jnp.int32, shape, 0)
                same = across_rows == lax.broadcasted_iota(jnp.int32, shape, 1)
                count = counts[2 * chunk + side].astype(jnp.float32)
                part = part - jnp.where(same, count, 0.0)
            out[number, 0, 2 * chunk + side] = part

    def lag_of(turn):
        return turn if turn == 0 else jnp.where(z == 0, 3 - turn, turn)

    def near_gram(turn, *places):
        lag = lag_of(turn)
        for place in places:
            gram(plane_behind(lag) * 4 + y * 2 + k, place, 4 * lag, turn == 0)

    def near_beside(turn, *places):
        lag = lag_of(turn)
        number = 4 * lag - swap
        source = plane_behind(lag) * 4 + y * 2 + 1 - k
        for place in places:

            @pl.when((number >= 0) & (number < out.shape[0]))
            def _():
                arrive2(source, turn_of(source, place))
                gram(source, place, number)

    def cross_gram(*places):
        for place in places:
            for lag, source in enumerate(cross):
                gram(source, place, 4 * lag + 2)

    def cross_beside(*places):
        for place in places:
            for lag, source in enumerate(cross):
                arrive2(source + swap, turn_of(source, place))
                gram(source + swap, place, 4 * lag + 2 - swap)

    for part in range(parts):
        start(z < top, move1(me, part, 0, up, True))
        start(z > 0, move1(me, part, 1, down, True))
        start(None, move1(me, part, 2, across, True))
        start(None, move1(me, part, 3, beside, True))
    mask(0)
    local[0].wait()
    mask(1)
    mask(2)
    mask(3)
    scales()
    column(1, inner)
    for some in ([0], list(range(1, parts))):
        column(1, edge, some)
        sideways(0, edge, some)
    column(2, inner)
    sideways(0, inner)
    finish(0)
    column_rest()
    start(edge, ship(0))
    column(2, edge)
    column(3, inner, [0])
    passing(0, z == 1)
    sideways(1, z == 1)
    column(3, inner, [1, 2])
    sideways(1, z != 1)
    finish(1)
    own_across(0)
    passing(1, z == 1)
    relay(0, 0, inner)
    passing(0, z == 2)
    sideways(2)
    finish(2)
    start(edge, ship(1))
    relay(1, 0, z == 2)
    passing(1, z == 2)
    relay(0, 0, edge)
    column(3, edge, [parts - 1])
    sideways(3, inner)
    relay(0, 1, z == 1)
    finish(3, inner)
    own_across(1)
    relay(0, 1, z == 2)
    near_gram(0, 0, 1, 3)
    relay(1, 0, edge)
    passing(2, inner)
    relay(1, 0, z == 1)
    near_beside(0, 0, 1, 3)
    relay(0, 1, edge)
    near_gram(1, 0)
    relay(2, 0, z == 2)
    relay(1, 1, z == 1)
    relay(2, 0, z == 1)
    relay(2, 0, edge)
    near_gram(1, 1)
    near_beside(1, 0)
    passing(3, (z == 1) & (y == 1))
    own_across(2)
    outside()
    relay(3, 0, z == 2)
    near_beside(1, 1)
    relay(1, 1, edge)
    near_gram(2, 0)
    relay(2, 1, z == 1)
    relay(1, 1, z == 2)
    near_beside(2, 0)
    relay(3, 0, (z == 3) | ((z == 0) & (y == 1)))
    cross_over(0)
    sideways(3, edge, [parts - 1])
    own_across(3, inner)
    relay(3, 1, z == 1)
    passing(3, (z == 1) & (y == 0))
    outside_rest()
    relay(2, 1, z == 2)
    relay(3, 1, z == 2)
    relay(2, 1, z == 3)
    returned((z == 3) | ((z == 0) & (y == 0)))
    cross_over(1)
    cross_gram(0)
    relay(2, 1, z == 0)
    cross_beside(0)
    near_gram(2, 1)
    near_beside(2, 1)
    relay(3, 1, edge)
    near_gram(2, 3)
    cross_over(2)
    cross_gram(1)
    cross_beside(1)
    near_beside(2, 3)
    relay(3, 0, (z == 0) & (y == 0))
    near_gram(1, 3)
    near_beside(1, 3)
    returned((z == 0) & (y == 1))
    near_gram(0, 2)
    near_gram(1, 2)
    near_gram(2, 2)
    near_beside(1, 2)
    near_beside(2, 2)
    cross_over(3)
    cross_gram(2, 3)
    near_beside(0, 2)
    cross_beside(2, 3)
    for condition, copy in pending:
        if condition is None:
            copy.wait_send()
        else:
            pl.when(condition)(copy.wait_send)


def exchange(vectors, values, samples, counts, snps, scores):
    devices = lax.axis_size("panel")
    piece, depth = vectors.shape
    blocks, snp_rows, width = scores.shape[1:]
    row_total = devices * piece
    pair_rows = 4 * piece
    parts = 3
    chunks = blocks // 2
    rounds = ROUNDS + 1
    hbm = pl.BlockSpec(memory_space=pltpu.HBM)
    operands = [counts, snps, vectors, values, samples.reshape(devices, width), scores]
    return pl.pallas_call(
        exchange_kernel,
        out_shape=[
            jax.ShapeDtypeStruct((rounds, 1, blocks, width, width), jnp.float32),
            jax.ShapeDtypeStruct((rounds, width, width), jnp.float32),
        ],
        in_specs=[hbm] * len(operands),
        out_specs=[pl.BlockSpec(memory_space=pltpu.VMEM)] * 2,
        scratch_shapes=[
            pltpu.SMEM((blocks,), jnp.int32),
            pltpu.SMEM((blocks,), jnp.int32),
            pltpu.VMEM((piece,), jnp.bfloat16),
            pltpu.VMEM((devices, width), jnp.bfloat16),
            pltpu.VMEM((devices, row_total, width), jnp.bfloat16),
            pltpu.VMEM((devices, 1, pair_rows), jnp.float32),
            pltpu.VMEM((chunks, 2 * width, pair_rows), jnp.bfloat16),
            pltpu.VMEM((row_total, depth), jnp.bfloat16),
            pltpu.VMEM((blocks + 2, snp_rows, width), jnp.bfloat16),
            pltpu.VMEM((chunks + 1, snp_rows, 2 * width), jnp.bfloat16),
            pltpu.SemaphoreType.DMA((5,)),
            pltpu.SemaphoreType.DMA((chunks,)),
            pltpu.SemaphoreType.DMA((2,)),
            pltpu.SemaphoreType.DMA((3,)),
            pltpu.SemaphoreType.DMA((devices, parts)),
            pltpu.SemaphoreType.DMA((devices, chunks)),
        ],
        compiler_params=pltpu.CompilerParams(
            collective_id=0, has_side_effects=True, vmem_limit_bytes=EXCHANGE_LIMIT
        ),
    )(*[pltpu.with_memory_space_constraint(operand, pltpu.HBM) for operand in operands])


def per_device(eig_vectors, eig_values, eig_count, snp_count, zscores, samples):
    devices = lax.axis_size("panel")
    spacing = max(1, devices // 32)
    panels = devices // spacing
    slot_index = lax.axis_index("panel")
    panel_index = slot_index // spacing
    group_index = slot_index % spacing
    blocks_here, snp_rows, panel_width = zscores.shape[1:]
    if spacing == 1 and panels == 2 * ROUNDS and blocks_here == panels // 2:
        raw, scale = exchange(eig_vectors, eig_values, samples, eig_count, snp_count, zscores)
        return raw * scale[:, None, None]
    counts = lax.dynamic_slice_in_dim(eig_count, group_index * blocks_here, blocks_here)
    snps = lax.dynamic_slice_in_dim(snp_count, group_index * blocks_here, blocks_here)
    rounds = jnp.arange(ROUNDS + 1, dtype=jnp.int32)
    partners = (panel_index - rounds) % panels
    scales = samples.astype(jnp.float32).reshape(panels, panel_width)
    own_scale = lax.dynamic_index_in_dim(scales, panel_index, 0, keepdims=False)
    scale = 1.0 / jnp.sqrt(own_scale[None, :, None] * scales[partners][:, None, :])
    members = [[g + spacing * i for i in range(panels)] for g in range(spacing)]
    gather = functools.partial(
        lax.all_gather, axis_name="panel", axis_index_groups=members if spacing > 1 else None
    )
    vectors = gather(eig_vectors, tiled=True)
    values = gather(eig_values, tiled=True)
    projected = project(vectors, zscores, counts, snps)
    held = gather(projected)
    weighted = (projected.astype(jnp.float32) / values.astype(jnp.float32)[:, None]).astype(
        jnp.bfloat16
    )
    return grams(weighted, held, scale, partners, counts)


def solution(mesh):
    placed = (
        P(("groups", "panel"), None),
        P(("groups", "panel")),
        P("groups"),
        P("groups"),
        P(("groups", "panel"), None, None, None),
        P("groups"),
    )
    return jax.shard_map(
        per_device,
        mesh=mesh,
        in_specs=placed,
        out_specs=P(None, ("groups", "panel"), None, None, None),
        check_vma=False,
    )
```

```python
import functools

import jax
import jax.numpy as jnp
from jax import lax
from jax.experimental import pallas as pl
from jax.experimental.pallas import tpu as pltpu
from jax.sharding import PartitionSpec as P

ROUNDS = 8
LIMIT = 56 * 1024 * 1024
EXCHANGE_LIMIT = 36 * 1024 * 1024
PUT_LIMIT = 1024 * 1024


def place_masked(snps, scores, pair, store):
    width = scores.shape[-1]
    for side in range(2):
        block = 2 * pair + side
        rows = lax.broadcasted_iota(jnp.int32, scores.shape[-2:], 0)
        part = jnp.where(rows < snps[block], scores[side].astype(jnp.float32), 0.0)
        store[:, side * width : (side + 1) * width] = part.astype(jnp.bfloat16)


def project_rows(vectors, masked, first_count):
    both = jnp.dot(vectors, masked, preferred_element_type=jnp.float32)
    width = both.shape[1] // 2
    rows = lax.broadcasted_iota(jnp.int32, (both.shape[0], width), 0)
    return jnp.where(rows < first_count, both[:, :width], both[:, width:]).astype(jnp.bfloat16)


def project_kernel(counts, snps, vectors, scores, out, masked):
    pair = pl.program_id(0)
    place_masked(snps, scores.at[0], pair, masked)
    out[...] = project_rows(vectors[...], masked[...], counts[2 * pair])


def project(vectors, scores, counts, snps):
    row_total, depth = vectors.shape
    blocks, snp_rows, width = scores.shape[1:]
    pair_rows = 2 * row_total // blocks
    return pl.pallas_call(
        project_kernel,
        out_shape=jax.ShapeDtypeStruct((row_total, width), jnp.bfloat16),
        grid_spec=pltpu.PrefetchScalarGridSpec(
            num_scalar_prefetch=2,
            grid=(blocks // 2,),
            in_specs=[
                pl.BlockSpec((pair_rows, depth), lambda b, *_: (b, 0)),
                pl.BlockSpec((1, 2, snp_rows, width), lambda b, *_: (0, b, 0, 0)),
            ],
            out_specs=pl.BlockSpec((pair_rows, width), lambda b, *_: (b, 0)),
            scratch_shapes=[pltpu.VMEM((snp_rows, 2 * width), jnp.bfloat16)],
        ),
        compiler_params=pltpu.CompilerParams(vmem_limit_bytes=LIMIT),
    )(counts, snps, vectors, scores)


def gram_kernel(counts, slots, weighted, panels, scale, out):
    pair = pl.program_id(0)
    width = weighted.shape[1]
    left = weighted[...].astype(jnp.float32)
    rows = lax.broadcasted_iota(jnp.int32, left.shape, 0)
    first = rows < counts[2 * pair]
    left = jnp.concatenate([jnp.where(first, left, 0.0).T, jnp.where(first, 0.0, left).T], axis=0)
    left = left.astype(jnp.bfloat16)
    shape = (width, width)
    same = lax.broadcasted_iota(jnp.int32, shape, 0) == lax.broadcasted_iota(jnp.int32, shape, 1)
    for index in range(out.shape[0]):
        both = jnp.dot(left, panels[slots[index]], preferred_element_type=jnp.float32)
        for side in range(2):
            gram = both[side * width : (side + 1) * width]
            if index == 0:
                count = counts[2 * pair + side].astype(jnp.float32)
                gram = gram - jnp.where(same, count, 0.0)
            out[index, 0, side] = gram * scale[index]


def grams(weighted, panels, scale, slots, counts):
    blocks = counts.shape[0]
    rounds, width = scale.shape[:2]
    pair_rows = 2 * weighted.shape[0] // blocks
    return pl.pallas_call(
        gram_kernel,
        out_shape=jax.ShapeDtypeStruct((rounds, 1, blocks, width, width), jnp.float32),
        grid_spec=pltpu.PrefetchScalarGridSpec(
            num_scalar_prefetch=2,
            grid=(blocks // 2,),
            in_specs=[
                pl.BlockSpec((pair_rows, width), lambda b, *_: (b, 0)),
                pl.BlockSpec((panels.shape[0], pair_rows, width), lambda b, *_: (0, b, 0)),
                pl.BlockSpec(scale.shape, lambda b, *_: (0, 0, 0)),
            ],
            out_specs=pl.BlockSpec((rounds, 1, 2, width, width), lambda b, *_: (0, 0, b, 0, 0)),
        ),
        compiler_params=pltpu.CompilerParams(vmem_limit_bytes=LIMIT),
    )(counts, slots, weighted, panels, scale)


def exchange_kernel(all_counts, all_snps, own, own_values, samples, scores, out, counts, snps,
                    flat_values, units, scale, held, values, left, store, raw, masked, here, load, shipped,
                    sent, recv1, recv2, recv3):
    line = lax.axis_size("panel") // 4
    me = lax.axis_index("panel")
    z = me // 4
    y = (me // 2) % 2
    k = me % 2
    piece = own.shape[0]
    pair_rows = 4 * piece
    parts = recv1.shape[1]
    part_rows = piece // (parts - 1)
    chunks = recv2.shape[1]
    top = line - 1
    inner = (z > 0) & (z < top)
    edge = (z == 0) | (z == top)
    up, down, across, beside = me + 4, me - 4, me + 2 - 4 * y, me + 1 - 2 * k
    inward = jnp.where(z == 0, up, down)
    outward = jnp.where(z == 1, down, up)
    pending = []
    pieces = []

    def order(plane, step):
        near = jnp.minimum(plane, top - plane)
        nearest = jnp.where(step > 2 * near, step, (near + (step + 1) // 2 * (1 - 2 * (step % 2))))
        return jnp.where(plane > top - plane, top - nearest, nearest)

    loads = []
    for step in range(line):
        pair = pl.ds(2 * order(z, step), 2)
        loads.append(
            pltpu.make_async_copy(scores.at[0, pair], raw.at[pl.ds(2 * step, 2)], load.at[step])
        )
    local = [
        pltpu.make_async_copy(own, store.at[pl.ds(me * piece, piece)], here.at[0]),
        pltpu.make_async_copy(own_values, flat_values, here.at[1]),
        pltpu.make_async_copy(all_counts, counts, here.at[2]),
        pltpu.make_async_copy(all_snps, snps, here.at[3]),
        pltpu.make_async_copy(samples, units, here.at[4]),
    ]
    for copy in local + loads:
        copy.start()

    barrier = pltpu.get_barrier_semaphore()

    def greet(target):
        pl.semaphore_signal(
            barrier, inc=1, device_id={"panel": target}, device_id_type=pl.DeviceIdType.MESH
        )

    pl.when(z < top)(functools.partial(greet, up))
    pl.when(z > 0)(functools.partial(greet, down))
    for target in (across, beside):
        greet(target)
    for copy in local[1:]:
        copy.wait()
    spot = lax.broadcasted_iota(jnp.int32, (piece, pair_rows), 1) - lax.rem(me, 4) * piece
    hot = jnp.where(spot == lax.broadcasted_iota(jnp.int32, spot.shape, 0), 1.0, 0.0)
    ride = jnp.broadcast_to(flat_values[...].astype(jnp.float32).reshape(1, piece), (8, piece))
    ride = jnp.dot(
        ride.astype(jnp.bfloat16), hot.astype(jnp.bfloat16), preferred_element_type=jnp.float32
    )
    values[me] = ride[0:1]
    pl.semaphore_wait(barrier, jnp.where(inner, 4, 3))

    def start(condition, copy, group=None):
        if condition is None:
            copy.start()
        else:
            pl.when(condition)(copy.start)
        (pending if group is None else group).append((condition, copy))

    def drain(group):
        for condition, copy in group:
            wait(condition, copy.wait_send)
        group.clear()

    def remote(source, target, send, recv, device):
        return pltpu.make_async_remote_copy(
            src_ref=source,
            dst_ref=target,
            send_sem=send,
            recv_sem=recv,
            device_id={"panel": device},
            device_id_type=pl.DeviceIdType.MESH,
        )

    def move1(source, part, way, target, first=False):
        sems = sent.at[0], recv1.at[source, part]
        if part == parts - 1:
            return remote(values.at[source], values.at[source], *sems, target)
        rows = pl.ds(source * piece + part * part_rows, part_rows)
        origin = own.at[pl.ds(part * part_rows, part_rows)] if first else store.at[rows]
        return remote(origin, store.at[rows], *sems, target)

    def arrive1(source, part):
        move1(source, part, 0, beside).wait_recv()

    def move2(source, chunk, way, target):
        block = held.at[source, pl.ds(chunk * pair_rows, pair_rows)]
        return remote(block, block, sent.at[1], recv2.at[source, chunk], target)

    def half2(source, chunk, half, target):
        rows = pl.ds(chunk * pair_rows + half * (pair_rows // 2), pair_rows // 2)
        block = held.at[source, rows]
        arrival = recv3.at[source] if half else recv2.at[source, chunk]
        return remote(block, block, sent.at[1], arrival, target)

    def give2(step, condition, source, chunk, target, some=range(2)):
        if step < top:
            start(condition, move2(source, chunk, 0, target))
        else:
            for half in some:
                start(condition, half2(source, chunk, half, target))

    def take2(step, condition, source, chunk, onward=()):
        if step < top:
            wait(condition, arrive2, source, chunk)
            for where, target in onward:
                give2(step, where, source, chunk, target)
        else:
            for half in range(2):
                wait(condition, half2(source, chunk, half, beside).wait_recv)
                for where, target in onward:
                    give2(step, where, source, chunk, target, [half])

    def arrive2(source, chunk):
        move2(source, chunk, 0, beside).wait_recv()

    def both(a, b):
        return b if a is None else a & b

    def column(step, condition, some=None):
        plane = order(z, step)
        source = plane * 4 + y * 2 + k
        for part in range(parts) if some is None else some:
            wait(condition, arrive1, source, part)
            if step < top or part == parts - 1:
                start(condition & (plane < z) & (z < top), move1(source, part, 0, up), pieces)
                held_back = (z == 2) if step == 1 and part > 0 else (z < 0)
                start(condition & (plane > z) & (z > 0) & ~held_back, move1(source, part, 1, down), pieces)
            if step == 1:
                start(condition & edge, move1(source, part, 2, across), pieces)
            else:
                start(condition, move1(source, part, 2, across), pieces)
            start(condition, move1(source, part, 3, beside), pieces)

    def column_rest():
        for part in range(1, parts):
            start(z == 2, move1(me + 4, part, 1, down), pieces)

    def passing(step, condition):
        source = me + 4
        take2(step, condition, source, order(z + 1, step), [(condition, down)])

    def sideways(step, condition=None, some=None):
        source = order(z, step) * 4 + 2 - 2 * y + k
        for part in range(parts) if some is None else some:
            wait(condition, arrive1, source, part)
            start(condition, move1(source, part, 3, beside), pieces)
            if step == 0:
                start(both(condition, edge), move1(source, part, 0, inward), pieces)

    def mask(step):
        loads[step].wait()
        place_masked(snps, raw.at[pl.ds(2 * step, 2)], order(z, step), masked.at[step])

    def wait(condition, arrive, *where):
        if condition is None:
            arrive(*where)
        else:
            pl.when(condition)(functools.partial(arrive, *where))

    def beside_pieces(step, condition, some):
        plane = order(z, step)
        for source in (plane * 4 + y * 2 + 1 - k, plane * 4 + 2 - 2 * y + 1 - k):
            for part in some:
                wait(condition, arrive1, source, part)

    def compute(step):
        plane = order(z, step)
        rows = pl.ds(plane * pair_rows, pair_rows)
        held[me, rows] = project_rows(store[rows], masked[step], counts[2 * plane])

    def finish(step, condition=None):
        plane = order(z, step)
        beside_pieces(step, condition, range(parts))
        wait(condition, compute, step)
        give2(step, both(condition, z < top), me, plane, up)
        give2(step, (z == 2) if step == top else (z >= 2), me, plane, down)
        start(both(condition, k == 0), move2(me, plane, 3, beside))
        wait(condition, weigh, plane)

    def ship(half):
        block = 2 * order(z, top) + half
        return remote(
            scores.at[0, pl.ds(block, 1)],
            raw.at[pl.ds(2 * line + half, 1)],
            sent.at[2],
            shipped.at[half],
            inward,
        )

    def compute_outside():
        plane = order(z, top)
        for half in range(2):
            ship(half).wait_recv()
        place_masked(snps, raw.at[pl.ds(2 * line, 2)], plane, masked.at[line])
        rows = pl.ds(plane * pair_rows, pair_rows)
        held[outward, rows] = project_rows(store[rows], masked[line], counts[2 * plane])

    def outside():
        plane = order(z, top)
        pl.when(inner)(compute_outside)
        for half in range(2):
            give2(top, inner, outward, plane, up, [half])
            give2(top, inner & ~late_return, outward, plane, down, [half])
            give2(top, z == 1, outward, plane, across, [half])
        start(z == 1, move2(outward, plane, 3, beside))

    late_return = (z == 1) & (y == 1)

    def outside_rest():
        give2(top, late_return, outward, order(z, top), down)

    def returned(condition):
        plane = order(z, top)
        beside_pieces(top, condition, [parts - 1])
        take2(top, condition, me, plane, [(condition & (y == 0), across)])
        start(condition & (k == 0), move2(me, plane, 3, beside))
        wait(condition, weigh, plane)

    def weigh(index):
        rows = pl.ds(index * pair_rows, pair_rows)
        row = values[4 * index] + values[4 * index + 1]
        row = row + (values[4 * index + 2] + values[4 * index + 3])
        flat = held[me, rows].astype(jnp.float32).T / row
        first = lax.broadcasted_iota(jnp.int32, flat.shape, 1) < counts[2 * index]
        both = jnp.concatenate([jnp.where(first, flat, 0.0), jnp.where(first, 0.0, flat)], axis=0)
        left[index] = both.astype(jnp.bfloat16)

    def scales():
        table = units[...].astype(jnp.float32)
        panels = lax.broadcasted_iota(jnp.int32, table.shape, 0)

        def row(panel):
            return jnp.sum(jnp.where(panels == panel, table, 0.0), axis=0, keepdims=True)

        width = table.shape[1]
        mine = jnp.broadcast_to(row(me), (width, width)).T
        for number in range(out.shape[0]):
            partner = lax.rem(me - number + 4 * line, 4 * line)
            scale[number] = 1.0 / jnp.sqrt(mine * row(partner))

    def plane_behind(lag):
        return lax.rem(z - lag + line, line)

    def own_across(step, condition=None):
        give2(step, both(condition, y == 0), me, order(z, step), across)

    def relay(step, turn, condition=None):
        lag = jnp.where(z == 0, 2 - turn, 1 + turn)
        plane = plane_behind(lag)
        source = plane * 4 + y * 2 + k
        chunk = order(plane, step)
        onward = [
            (both(condition, (lag == 1) & inner), up),
            (both(condition, (lag == 2) & (z == 1)), down),
            (both(condition, (lag == 1) | (y == 1)), across),
        ]
        take2(step, condition, source, chunk, onward)
        start(both(condition, (lag == 1) | (k == 1)), move2(source, chunk, 3, beside))

    cross = [plane_behind(lag + 1 - y) * 4 + (1 - y) * 2 + k for lag in range(2)]
    swap = 1 - 2 * k

    def cross_over(step):
        for source in cross:
            chunk = order(source // 4, step)
            take2(step, None, source, chunk)
            start(None, move2(source, chunk, 3, beside))

    def turn_of(source, place):
        plane = source // 4
        late = sum(jnp.where(order(plane, step) == order(z, top), step, 0) for step in range(line))
        if place == 2:
            step = late
        else:
            rank = min(place, 2)
            step = rank + jnp.where(rank >= late, 1, 0)
        return order(plane, jnp.where(edge, step, place))

    def gram(source, step, number, own_panel=False):
        chunk = turn_of(source, step)
        rows = pl.ds(chunk * pair_rows, pair_rows)
        both = jnp.dot(left[chunk], held[source, rows], preferred_element_type=jnp.float32)
        width = both.shape[1]
        for side in range(2):
            part = both[side * width : (side + 1) * width]
            if own_panel:
                shape = (width, width)
                across_rows = lax.broadcasted_iota(jnp.int32, shape, 0)
                same = across_rows == lax.broadcasted_iota(jnp.int32, shape, 1)
                count = counts[2 * chunk + side].astype(jnp.float32)
                part = part - jnp.where(same, count, 0.0)
            out[number, 0, 2 * chunk + side] = part * scale[number]

    def lag_of(turn):
        return turn if turn == 0 else jnp.where(z == 0, 3 - turn, turn)

    def near_gram(turn, *places, condition=None):
        lag = lag_of(turn)
        source = plane_behind(lag) * 4 + y * 2 + k
        for place in places:
            wait(condition, gram, source, place, 4 * lag, turn == 0)

    def near_beside(turn, *places, condition=None):
        lag = lag_of(turn)
        number = 4 * lag - swap
        source = plane_behind(lag) * 4 + y * 2 + 1 - k
        for place in places:

            @pl.when(both(condition, (number >= 0) & (number < out.shape[0])))
            def _():
                arrive2(source, turn_of(source, place))
                gram(source, place, number)

    def cross_gram(*places):
        for place in places:
            for lag, source in enumerate(cross):
                gram(source, place, 4 * lag + 2)

    def cross_beside(*places):
        for place in places:
            for lag, source in enumerate(cross):
                arrive2(source + swap, turn_of(source, place))
                gram(source + swap, place, 4 * lag + 2 - swap)

    for part in range(parts):
        start(z < top, move1(me, part, 0, up, True), pieces)
        start(z > 0, move1(me, part, 1, down, True), pieces)
        start(None, move1(me, part, 2, across, True), pieces)
        start(None, move1(me, part, 3, beside, True), pieces)
    mask(0)
    local[0].wait()
    mask(1)
    mask(2)
    mask(3)
    scales()
    for some in ([0], list(range(1, parts))):
        column(1, inner, some)
        column(2, inner, some)
        column(1, edge, some)
        sideways(0, edge, some)
    sideways(0, inner)
    finish(0)
    column_rest()
    column(2, edge)
    column(3, inner, [0])
    passing(0, z == 1)
    sideways(1, z == 1)
    column(3, inner, [1, 2])
    sideways(1, z != 1)
    finish(1)
    start(edge, ship(0))
    own_across(0)
    passing(1, z == 1)
    relay(0, 0, inner)
    passing(0, z == 2)
    sideways(2)
    finish(2)
    start(edge, ship(1))
    passing(1, z == 2)
    relay(1, 0, z == 2)
    relay(0, 0, edge)
    column(3, edge, [parts - 1])
    sideways(3, inner)
    relay(0, 1, z == 1)
    finish(3, inner)
    own_across(1)
    relay(0, 1, z == 2)
    near_gram(0, 0, 1, 3)
    relay(1, 0, edge)
    passing(2, inner)
    relay(1, 0, z == 1)
    near_beside(0, 0, 1, 3)
    relay(0, 1, edge)
    near_gram(1, 0)
    relay(2, 0, z == 2)
    relay(1, 1, z == 1)
    relay(2, 0, z == 1)
    relay(2, 0, edge)
    near_gram(1, 1)
    near_beside(1, 0)
    passing(3, (z == 1) & (y == 1))
    own_across(2)
    outside()
    relay(3, 0, z == 2)
    near_beside(1, 1)
    relay(1, 1, edge)
    near_gram(2, 0)
    relay(2, 1, z == 1)
    relay(1, 1, z == 2)
    near_beside(2, 0)
    relay(3, 0, (z == 3) | ((z == 0) & (y == 1)))
    cross_over(0)
    sideways(3, edge, [parts - 1])
    own_across(3, inner)
    relay(3, 1, z == 1)
    passing(3, (z == 1) & (y == 0))
    outside_rest()
    relay(2, 1, z == 2)
    relay(3, 1, z == 2)
    relay(2, 1, z == 3)
    returned((z == 3) | ((z == 0) & (y == 0)))
    cross_over(1)
    cross_gram(0)
    relay(2, 1, z == 0)
    cross_beside(0)
    near_gram(2, 1)
    near_beside(2, 1)
    relay(3, 1, edge)
    near_gram(2, 3)
    last_return = (z == 0) & (y == 1)
    for turn in range(3):
        near_gram(turn, 2, condition=~last_return)
    for turn in range(3):
        near_beside(turn, 2, condition=~last_return)
    drain(pieces)
    cross_over(2)
    cross_gram(1)
    cross_beside(1)
    near_beside(2, 3)
    relay(3, 0, (z == 0) & (y == 0))
    near_gram(1, 3)
    near_beside(1, 3)
    returned(last_return)
    for turn in range(3):
        near_gram(turn, 2, condition=last_return)
    for turn in range(3):
        near_beside(turn, 2, condition=last_return)
    cross_over(3)
    cross_gram(2, 3)
    cross_beside(2, 3)
    drain(pending)


def exchange(vectors, values, samples, counts, snps, scores):
    devices = lax.axis_size("panel")
    piece, depth = vectors.shape
    blocks, snp_rows, width = scores.shape[1:]
    row_total = devices * piece
    pair_rows = 4 * piece
    parts = 3
    chunks = blocks // 2
    rounds = ROUNDS + 1
    hbm = pl.BlockSpec(memory_space=pltpu.HBM)
    operands = [counts, snps, vectors, values, samples.reshape(devices, width), scores]
    return pl.pallas_call(
        exchange_kernel,
        out_shape=jax.ShapeDtypeStruct((rounds, 1, blocks, width, width), jnp.float32),
        in_specs=[hbm] * len(operands),
        out_specs=pl.BlockSpec(memory_space=pltpu.VMEM),
        scratch_shapes=[
            pltpu.SMEM((blocks,), jnp.int32),
            pltpu.SMEM((blocks,), jnp.int32),
            pltpu.VMEM((piece,), jnp.bfloat16),
            pltpu.VMEM((devices, width), jnp.bfloat16),
            pltpu.VMEM((rounds, width, width), jnp.float32),
            pltpu.VMEM((devices, row_total, width), jnp.bfloat16),
            pltpu.VMEM((devices, 1, pair_rows), jnp.float32),
            pltpu.VMEM((chunks, 2 * width, pair_rows), jnp.bfloat16),
            pltpu.VMEM((row_total, depth), jnp.bfloat16),
            pltpu.VMEM((blocks + 2, snp_rows, width), jnp.bfloat16),
            pltpu.VMEM((chunks + 1, snp_rows, 2 * width), jnp.bfloat16),
            pltpu.SemaphoreType.DMA((5,)),
            pltpu.SemaphoreType.DMA((chunks,)),
            pltpu.SemaphoreType.DMA((2,)),
            pltpu.SemaphoreType.DMA((3,)),
            pltpu.SemaphoreType.DMA((devices, parts)),
            pltpu.SemaphoreType.DMA((devices, chunks)),
            pltpu.SemaphoreType.DMA((devices,)),
        ],
        compiler_params=pltpu.CompilerParams(
            collective_id=0, has_side_effects=True, vmem_limit_bytes=EXCHANGE_LIMIT
        ),
    )(*[pltpu.with_memory_space_constraint(operand, pltpu.HBM) for operand in operands])


def put_kernel(source, target, done):
    copies = [
        pltpu.make_async_copy(source.at[index], target.at[index], done.at[index])
        for index in range(source.shape[0])
    ]
    for copy in copies:
        copy.start()
    for copy in copies:
        copy.wait()


def put_out(array):
    return pl.pallas_call(
        put_kernel,
        out_shape=jax.ShapeDtypeStruct(array.shape, array.dtype),
        in_specs=[pl.BlockSpec(memory_space=pl.ANY)],
        out_specs=pl.BlockSpec(memory_space=pl.ANY),
        scratch_shapes=[pltpu.SemaphoreType.DMA((array.shape[0],))],
        compiler_params=pltpu.CompilerParams(vmem_limit_bytes=PUT_LIMIT),
    )(array)


def per_device(eig_vectors, eig_values, eig_count, snp_count, zscores, samples):
    devices = lax.axis_size("panel")
    spacing = max(1, devices // 32)
    panels = devices // spacing
    slot_index = lax.axis_index("panel")
    panel_index = slot_index // spacing
    group_index = slot_index % spacing
    blocks_here, snp_rows, panel_width = zscores.shape[1:]
    if spacing == 1 and panels == 2 * ROUNDS and blocks_here == panels // 2:
        return put_out(
            exchange(eig_vectors, eig_values, samples, eig_count, snp_count, zscores)
        )
    counts = lax.dynamic_slice_in_dim(eig_count, group_index * blocks_here, blocks_here)
    snps = lax.dynamic_slice_in_dim(snp_count, group_index * blocks_here, blocks_here)
    rounds = jnp.arange(ROUNDS + 1, dtype=jnp.int32)
    partners = (panel_index - rounds) % panels
    scales = samples.astype(jnp.float32).reshape(panels, panel_width)
    own_scale = lax.dynamic_index_in_dim(scales, panel_index, 0, keepdims=False)
    scale = 1.0 / jnp.sqrt(own_scale[None, :, None] * scales[partners][:, None, :])
    members = [[g + spacing * i for i in range(panels)] for g in range(spacing)]
    gather = functools.partial(
        lax.all_gather, axis_name="panel", axis_index_groups=members if spacing > 1 else None
    )
    vectors = gather(eig_vectors, tiled=True)
    values = gather(eig_values, tiled=True)
    projected = project(vectors, zscores, counts, snps)
    held = gather(projected)
    weighted = (projected.astype(jnp.float32) / values.astype(jnp.float32)[:, None]).astype(
        jnp.bfloat16
    )
    return grams(weighted, held, scale, partners, counts)


def solution(mesh):
    placed = (
        P(("groups", "panel"), None),
        P(("groups", "panel")),
        P("groups"),
        P("groups"),
        P(("groups", "panel"), None, None, None),
        P("groups"),
    )
    return jax.shard_map(
        per_device,
        mesh=mesh,
        in_specs=placed,
        out_specs=P(None, ("groups", "panel"), None, None, None),
        check_vma=False,
    )
```

```python
import functools

import jax
import jax.numpy as jnp
from jax import lax
from jax.experimental import pallas as pl
from jax.experimental.pallas import tpu as pltpu
from jax.sharding import PartitionSpec as P

ROUNDS = 8
LIMIT = 56 * 1024 * 1024
EXCHANGE_LIMIT = 36 * 1024 * 1024
PUT_LIMIT = 1024 * 1024


def place_masked(snps, scores, pair, store):
    width = scores.shape[-1]
    for side in range(2):
        block = 2 * pair + side
        rows = lax.broadcasted_iota(jnp.int32, scores.shape[-2:], 0)
        part = jnp.where(rows < snps[block], scores[side].astype(jnp.float32), 0.0)
        store[:, side * width : (side + 1) * width] = part.astype(jnp.bfloat16)


def project_rows(vectors, masked, first_count):
    both = jnp.dot(vectors, masked, preferred_element_type=jnp.float32)
    width = both.shape[1] // 2
    rows = lax.broadcasted_iota(jnp.int32, (both.shape[0], width), 0)
    return jnp.where(rows < first_count, both[:, :width], both[:, width:]).astype(jnp.bfloat16)


def project_kernel(counts, snps, vectors, scores, out, masked):
    pair = pl.program_id(0)
    place_masked(snps, scores.at[0], pair, masked)
    out[...] = project_rows(vectors[...], masked[...], counts[2 * pair])


def project(vectors, scores, counts, snps):
    row_total, depth = vectors.shape
    blocks, snp_rows, width = scores.shape[1:]
    pair_rows = 2 * row_total // blocks
    return pl.pallas_call(
        project_kernel,
        out_shape=jax.ShapeDtypeStruct((row_total, width), jnp.bfloat16),
        grid_spec=pltpu.PrefetchScalarGridSpec(
            num_scalar_prefetch=2,
            grid=(blocks // 2,),
            in_specs=[
                pl.BlockSpec((pair_rows, depth), lambda b, *_: (b, 0)),
                pl.BlockSpec((1, 2, snp_rows, width), lambda b, *_: (0, b, 0, 0)),
            ],
            out_specs=pl.BlockSpec((pair_rows, width), lambda b, *_: (b, 0)),
            scratch_shapes=[pltpu.VMEM((snp_rows, 2 * width), jnp.bfloat16)],
        ),
        compiler_params=pltpu.CompilerParams(vmem_limit_bytes=LIMIT),
    )(counts, snps, vectors, scores)


def gram_kernel(counts, slots, weighted, panels, scale, out):
    pair = pl.program_id(0)
    width = weighted.shape[1]
    left = weighted[...].astype(jnp.float32)
    rows = lax.broadcasted_iota(jnp.int32, left.shape, 0)
    first = rows < counts[2 * pair]
    left = jnp.concatenate([jnp.where(first, left, 0.0).T, jnp.where(first, 0.0, left).T], axis=0)
    left = left.astype(jnp.bfloat16)
    shape = (width, width)
    same = lax.broadcasted_iota(jnp.int32, shape, 0) == lax.broadcasted_iota(jnp.int32, shape, 1)
    for index in range(out.shape[0]):
        both = jnp.dot(left, panels[slots[index]], preferred_element_type=jnp.float32)
        for side in range(2):
            gram = both[side * width : (side + 1) * width]
            if index == 0:
                count = counts[2 * pair + side].astype(jnp.float32)
                gram = gram - jnp.where(same, count, 0.0)
            out[index, 0, side] = gram * scale[index]


def grams(weighted, panels, scale, slots, counts):
    blocks = counts.shape[0]
    rounds, width = scale.shape[:2]
    pair_rows = 2 * weighted.shape[0] // blocks
    return pl.pallas_call(
        gram_kernel,
        out_shape=jax.ShapeDtypeStruct((rounds, 1, blocks, width, width), jnp.float32),
        grid_spec=pltpu.PrefetchScalarGridSpec(
            num_scalar_prefetch=2,
            grid=(blocks // 2,),
            in_specs=[
                pl.BlockSpec((pair_rows, width), lambda b, *_: (b, 0)),
                pl.BlockSpec((panels.shape[0], pair_rows, width), lambda b, *_: (0, b, 0)),
                pl.BlockSpec(scale.shape, lambda b, *_: (0, 0, 0)),
            ],
            out_specs=pl.BlockSpec((rounds, 1, 2, width, width), lambda b, *_: (0, 0, b, 0, 0)),
        ),
        compiler_params=pltpu.CompilerParams(vmem_limit_bytes=LIMIT),
    )(counts, slots, weighted, panels, scale)


def exchange_kernel(all_counts, all_snps, own, own_values, samples, scores, out, counts, snps,
                    flat_values, units, scale, held, values, left, store, raw, masked, here, load, shipped,
                    sent, recv1, recv2, recv3):
    line = lax.axis_size("panel") // 4
    me = lax.axis_index("panel")
    z = me // 4
    y = (me // 2) % 2
    k = me % 2
    piece = own.shape[0]
    pair_rows = 4 * piece
    parts = recv1.shape[1]
    part_rows = piece // (parts - 1)
    chunks = recv2.shape[1]
    top = line - 1
    fine = top - 1
    inner = (z > 0) & (z < top)
    edge = (z == 0) | (z == top)
    up, down, across, beside = me + 4, me - 4, me + 2 - 4 * y, me + 1 - 2 * k
    inward = jnp.where(z == 0, up, down)
    outward = jnp.where(z == 1, down, up)
    pending = []
    pieces = []

    def order(plane, step):
        near = jnp.minimum(plane, top - plane)
        nearest = jnp.where(step > 2 * near, step, (near + (step + 1) // 2 * (1 - 2 * (step % 2))))
        return jnp.where(plane > top - plane, top - nearest, nearest)

    loads = []
    for step in range(line):
        pair = pl.ds(2 * order(z, step), 2)
        loads.append(
            pltpu.make_async_copy(scores.at[0, pair], raw.at[pl.ds(2 * step, 2)], load.at[step])
        )
    local = [
        pltpu.make_async_copy(own, store.at[pl.ds(me * piece, piece)], here.at[0]),
        pltpu.make_async_copy(own_values, flat_values, here.at[1]),
        pltpu.make_async_copy(all_counts, counts, here.at[2]),
        pltpu.make_async_copy(all_snps, snps, here.at[3]),
        pltpu.make_async_copy(samples, units, here.at[4]),
    ]
    barrier = pltpu.get_barrier_semaphore()

    def greet(target):
        pl.semaphore_signal(
            barrier, inc=1, device_id={"panel": target}, device_id_type=pl.DeviceIdType.MESH
        )

    pl.when(z < top)(functools.partial(greet, up))
    pl.when(z > 0)(functools.partial(greet, down))
    for target in (across, beside):
        greet(target)
    for copy in local + loads:
        copy.start()
    spot = lax.broadcasted_iota(jnp.int32, (piece, pair_rows), 1) - lax.rem(me, 4) * piece
    hot = jnp.where(spot == lax.broadcasted_iota(jnp.int32, spot.shape, 0), 1.0, 0.0)
    hot = hot.astype(jnp.bfloat16)
    pl.semaphore_wait(barrier, jnp.where(inner, 4, 3))

    def start(condition, copy, group=None):
        if condition is None:
            copy.start()
        else:
            pl.when(condition)(copy.start)
        (pending if group is None else group).append((condition, copy))

    def drain(group):
        for condition, copy in group:
            wait(condition, copy.wait_send)
        group.clear()

    def remote(source, target, send, recv, device):
        return pltpu.make_async_remote_copy(
            src_ref=source,
            dst_ref=target,
            send_sem=send,
            recv_sem=recv,
            device_id={"panel": device},
            device_id_type=pl.DeviceIdType.MESH,
        )

    def move1(source, part, way, target, first=False):
        sems = sent.at[0], recv1.at[source, part]
        if part == parts - 1:
            return remote(values.at[source], values.at[source], *sems, target)
        rows = pl.ds(source * piece + part * part_rows, part_rows)
        origin = own.at[pl.ds(part * part_rows, part_rows)] if first else store.at[rows]
        return remote(origin, store.at[rows], *sems, target)

    def arrive1(source, part):
        move1(source, part, 0, beside).wait_recv()

    def slot(source, target):
        return jnp.minimum(lax.rem(target - source + 4 * line, 4 * line), recv2.shape[0] - 1)

    def move2(source, chunk, way, target, sends=1):
        block = held.at[source, pl.ds(chunk * pair_rows, pair_rows)]
        return remote(block, block, sent.at[sends], recv2.at[slot(source, target), chunk], target)

    def half2(step, source, chunk, half, target):
        rows = pl.ds(chunk * pair_rows + half * (pair_rows // 2), pair_rows // 2)
        block = held.at[source, rows]
        place = slot(source, target)
        arrival = recv3.at[place, step - fine] if half else recv2.at[place, chunk]
        return remote(block, block, sent.at[1], arrival, target)

    def give2(step, condition, source, chunk, target, some=range(2)):
        if step < fine:
            start(condition, move2(source, chunk, 0, target, 3), pieces)
        else:
            for half in some:
                start(condition, half2(step, source, chunk, half, target))

    def take2(step, condition, source, chunk, onward=()):
        if step < fine:
            wait(condition, arrive2, source, chunk)
            for where, target in onward:
                give2(step, where, source, chunk, target)
        else:
            for half in range(2):
                wait(condition, half2(step, source, chunk, half, me).wait_recv)
                for where, target in onward:
                    give2(step, where, source, chunk, target, [half])

    def arrive2(source, chunk):
        move2(source, chunk, 0, me).wait_recv()

    def both(a, b):
        return b if a is None else a & b

    def column(step, condition, some=None):
        plane = order(z, step)
        source = plane * 4 + y * 2 + k
        for part in range(parts) if some is None else some:
            wait(condition, arrive1, source, part)
            if step < top or part == parts - 1:
                start(condition & (plane < z) & (z < top), move1(source, part, 0, up), pieces)
                held_back = (z == 2) if step == 1 and part > 0 else (z < 0)
                start(condition & (plane > z) & (z > 0) & ~held_back, move1(source, part, 1, down), pieces)
            if step == 1:
                start(condition & edge, move1(source, part, 2, across), pieces)
            else:
                start(condition, move1(source, part, 2, across), pieces)
            start(condition, move1(source, part, 3, beside), pieces)

    def column_rest():
        for part in range(1, parts):
            start(z == 2, move1(me + 4, part, 1, down), pieces)

    def passing(step, condition):
        source = me + 4
        take2(step, condition, source, order(z + 1, step), [(condition, down)])

    def sideways(step, condition=None, some=None):
        source = order(z, step) * 4 + 2 - 2 * y + k
        for part in range(parts) if some is None else some:
            wait(condition, arrive1, source, part)
            start(condition, move1(source, part, 3, beside), pieces)
            if step == 0:
                start(both(condition, edge), move1(source, part, 0, inward), pieces)

    def mask(step):
        loads[step].wait()
        place_masked(snps, raw.at[pl.ds(2 * step, 2)], order(z, step), masked.at[step])

    def wait(condition, arrive, *where):
        if condition is None:
            arrive(*where)
        else:
            pl.when(condition)(functools.partial(arrive, *where))

    def beside_pieces(step, condition, some):
        plane = order(z, step)
        for source in (plane * 4 + y * 2 + 1 - k, plane * 4 + 2 - 2 * y + 1 - k):
            for part in some:
                wait(condition, arrive1, source, part)

    def compute(step):
        plane = order(z, step)
        rows = pl.ds(plane * pair_rows, pair_rows)
        held[me, rows] = project_rows(store[rows], masked[step], counts[2 * plane])

    def finish(step, condition=None):
        plane = order(z, step)
        beside_pieces(step, condition, range(parts))
        wait(condition, compute, step)
        give2(step, both(condition, z < top), me, plane, up)
        give2(step, (z == 2) if step == top else (z >= 2), me, plane, down)
        start(both(condition, k == 0), move2(me, plane, 3, beside))
        wait(condition, weigh, plane)

    def ship(half):
        block = 2 * order(z, top) + half
        return remote(
            scores.at[0, pl.ds(block, 1)],
            raw.at[pl.ds(2 * line + half, 1)],
            sent.at[2],
            shipped.at[half],
            inward,
        )

    def compute_outside():
        plane = order(z, top)
        for half in range(2):
            ship(half).wait_recv()
        place_masked(snps, raw.at[pl.ds(2 * line, 2)], plane, masked.at[line])
        rows = pl.ds(plane * pair_rows, pair_rows)
        held[outward, rows] = project_rows(store[rows], masked[line], counts[2 * plane])

    def outside():
        plane = order(z, top)
        pl.when(inner)(compute_outside)
        for half in range(2):
            give2(top, inner, outward, plane, up, [half])
            give2(top, inner & ~late_return, outward, plane, down, [half])
            give2(top, z == 1, outward, plane, across, [half])
        start(z == 1, move2(outward, plane, 3, beside))

    late_return = (z == 1) & (y == 1)

    def outside_rest():
        give2(top, late_return, outward, order(z, top), down)

    def returned(condition):
        plane = order(z, top)
        beside_pieces(top, condition, [parts - 1])
        take2(top, condition, me, plane, [(condition & (y == 0), across)])
        start(condition & (k == 0), move2(me, plane, 3, beside))
        wait(condition, weigh, plane)

    def weigh(index):
        rows = pl.ds(index * pair_rows, pair_rows)
        row = values[4 * index] + values[4 * index + 1]
        row = row + (values[4 * index + 2] + values[4 * index + 3])
        flat = held[me, rows].astype(jnp.float32).T / row
        first = lax.broadcasted_iota(jnp.int32, flat.shape, 1) < counts[2 * index]
        both = jnp.concatenate([jnp.where(first, flat, 0.0), jnp.where(first, 0.0, flat)], axis=0)
        left[index] = both.astype(jnp.bfloat16)

    def scales():
        table = units[...].astype(jnp.float32)
        panels = lax.broadcasted_iota(jnp.int32, table.shape, 0)

        def row(panel):
            return jnp.sum(jnp.where(panels == panel, table, 0.0), axis=0, keepdims=True)

        width = table.shape[1]
        mine = jnp.broadcast_to(row(me), (width, width)).T
        for number in range(out.shape[0]):
            partner = lax.rem(me - number + 4 * line, 4 * line)
            scale[number] = 1.0 / jnp.sqrt(mine * row(partner))

    def plane_behind(lag):
        return lax.rem(z - lag + line, line)

    def own_across(step, condition=None):
        give2(step, both(condition, y == 0), me, order(z, step), across)

    def relay(step, turn, condition=None):
        lag = jnp.where(z == 0, 2 - turn, 1 + turn)
        plane = plane_behind(lag)
        source = plane * 4 + y * 2 + k
        chunk = order(plane, step)
        onward = [
            (both(condition, (lag == 1) & inner), up),
            (both(condition, (lag == 2) & (z == 1)), down),
            (both(condition, (lag == 1) | (y == 1)), across),
        ]
        take2(step, condition, source, chunk, onward)
        start(both(condition, (lag == 1) | (k == 1)), move2(source, chunk, 3, beside))

    cross = [plane_behind(lag + 1 - y) * 4 + (1 - y) * 2 + k for lag in range(2)]
    swap = 1 - 2 * k

    def cross_over(step):
        for source in cross:
            chunk = order(source // 4, step)
            take2(step, None, source, chunk)
            start(None, move2(source, chunk, 3, beside))

    def turn_of(source, place):
        plane = source // 4
        late = sum(jnp.where(order(plane, step) == order(z, top), step, 0) for step in range(line))
        if place == 2:
            step = late
        else:
            rank = min(place, 2)
            step = rank + jnp.where(rank >= late, 1, 0)
        return order(plane, jnp.where(edge, step, place))

    def gram(source, step, number, own_panel=False):
        chunk = turn_of(source, step)
        rows = pl.ds(chunk * pair_rows, pair_rows)
        both = jnp.dot(left[chunk], held[source, rows], preferred_element_type=jnp.float32)
        width = both.shape[1]
        for side in range(2):
            part = both[side * width : (side + 1) * width]
            if own_panel:
                shape = (width, width)
                across_rows = lax.broadcasted_iota(jnp.int32, shape, 0)
                same = across_rows == lax.broadcasted_iota(jnp.int32, shape, 1)
                count = counts[2 * chunk + side].astype(jnp.float32)
                part = part - jnp.where(same, count, 0.0)
            out[number, 0, 2 * chunk + side] = part * scale[number]

    def lag_of(turn):
        return turn if turn == 0 else jnp.where(z == 0, 3 - turn, turn)

    def near_gram(turn, *places, condition=None):
        lag = lag_of(turn)
        source = plane_behind(lag) * 4 + y * 2 + k
        for place in places:
            wait(condition, gram, source, place, 4 * lag, turn == 0)

    def near_beside(turn, *places, condition=None):
        lag = lag_of(turn)
        number = 4 * lag - swap
        source = plane_behind(lag) * 4 + y * 2 + 1 - k
        for place in places:

            @pl.when(both(condition, (number >= 0) & (number < out.shape[0])))
            def _():
                arrive2(source, turn_of(source, place))
                gram(source, place, number)

    def cross_gram(*places, condition=None):
        for place in places:
            for lag, source in enumerate(cross):
                wait(condition, gram, source, place, 4 * lag + 2)

    def cross_beside(*places, condition=None):
        def beside_gram(source, place, number):
            arrive2(source, turn_of(source, place))
            gram(source, place, number)

        for place in places:
            for lag, source in enumerate(cross):
                wait(condition, beside_gram, source + swap, place, 4 * lag + 2 - swap)

    for part in range(parts):
        if part == parts - 1:
            for copy in local[1:]:
                copy.wait()
            ride = flat_values[...].astype(jnp.float32).reshape(1, piece)
            ride = jnp.broadcast_to(ride, (8, piece)).astype(jnp.bfloat16)
            values[me] = jnp.dot(ride, hot, preferred_element_type=jnp.float32)[0:1]
        start(z < top, move1(me, part, 0, up, True), pieces)
        start(z > 0, move1(me, part, 1, down, True), pieces)
        start(None, move1(me, part, 2, across, True), pieces)
        start(None, move1(me, part, 3, beside, True), pieces)
    mask(0)
    local[0].wait()
    mask(1)
    mask(2)
    mask(3)
    scales()
    for some in ([0], list(range(1, parts))):
        column(1, inner, some)
        column(2, inner, some)
        column(1, edge, some)
        sideways(0, edge, some)
    sideways(0, inner)
    finish(0)
    column_rest()
    column(2, edge)
    column(3, inner, [0])
    passing(0, z == 1)
    sideways(1, z == 1)
    column(3, inner, [1, 2])
    sideways(1, z != 1)
    finish(1)
    start(edge, ship(0))
    own_across(0)
    passing(1, z == 1)
    relay(0, 0, inner)
    passing(0, z == 2)
    sideways(2)
    finish(2)
    start(edge, ship(1))
    passing(1, z == 2)
    relay(1, 0, z == 2)
    relay(0, 0, edge)
    column(3, edge, [parts - 1])
    sideways(3, inner)
    relay(0, 1, z == 1)
    finish(3, inner)
    own_across(1)
    relay(0, 1, z == 2)
    near_gram(0, 0, 1, 3)
    relay(1, 0, edge)
    passing(2, inner)
    relay(1, 0, z == 1)
    near_beside(0, 0, 1, 3)
    relay(0, 1, edge)
    near_gram(1, 0)
    relay(2, 0, z == 2)
    relay(1, 1, z == 1)
    relay(2, 0, z == 1)
    relay(2, 0, edge)
    near_gram(1, 1)
    near_beside(1, 0)
    passing(3, (z == 1) & (y == 1))
    own_across(2)
    outside()
    relay(3, 0, z == 2)
    near_beside(1, 1)
    relay(1, 1, edge)
    near_gram(2, 0)
    relay(2, 1, z == 1)
    relay(1, 1, z == 2)
    near_beside(2, 0)
    relay(3, 0, (z == 3) | ((z == 0) & (y == 1)))
    cross_over(0)
    sideways(3, edge, [parts - 1])
    own_across(3, inner)
    relay(3, 1, z == 1)
    passing(3, (z == 1) & (y == 0))
    outside_rest()
    relay(2, 1, z == 2)
    relay(3, 1, z == 2)
    relay(2, 1, z == 3)
    returned((z == 3) | ((z == 0) & (y == 0)))
    cross_over(1)
    cross_gram(0)
    relay(2, 1, z == 0)
    cross_beside(0)
    near_gram(2, 1)
    near_beside(2, 1)
    relay(3, 1, edge)
    near_gram(2, 3)
    last_return = (z == 0) & (y == 1)
    for turn in range(3):
        near_gram(turn, 2, condition=~last_return)
    for turn in range(3):
        near_beside(turn, 2, condition=~last_return)
    drain(pieces)
    cross_over(2)
    cross_gram(1)
    near_beside(2, 3)
    relay(3, 0, (z == 0) & (y == 0))
    near_gram(1, 3)
    cross_beside(1)
    returned(last_return)
    for turn in range(3):
        near_gram(turn, 2, condition=last_return)
    for turn in range(3):
        near_beside(turn, 2, condition=last_return)
    early = inner | ((z == 0) & (y == 0))
    cross_gram(2, condition=early)
    cross_over(3)
    cross_gram(2, condition=~early)
    cross_beside(2)
    cross_gram(3)
    near_beside(1, 3)
    cross_beside(3)
    drain(pending)


def exchange(vectors, values, samples, counts, snps, scores):
    devices = lax.axis_size("panel")
    piece, depth = vectors.shape
    blocks, snp_rows, width = scores.shape[1:]
    row_total = devices * piece
    pair_rows = 4 * piece
    parts = 3
    chunks = blocks // 2
    rounds = ROUNDS + 1
    hbm = pl.BlockSpec(memory_space=pltpu.HBM)
    operands = [counts, snps, vectors, values, samples.reshape(devices, width), scores]
    return pl.pallas_call(
        exchange_kernel,
        out_shape=jax.ShapeDtypeStruct((rounds, 1, blocks, width, width), jnp.float32),
        in_specs=[hbm] * len(operands),
        out_specs=pl.BlockSpec(memory_space=pltpu.VMEM),
        scratch_shapes=[
            pltpu.SMEM((blocks,), jnp.int32),
            pltpu.SMEM((blocks,), jnp.int32),
            pltpu.VMEM((piece,), jnp.bfloat16),
            pltpu.VMEM((devices, width), jnp.bfloat16),
            pltpu.VMEM((rounds, width, width), jnp.float32),
            pltpu.VMEM((devices, row_total, width), jnp.bfloat16),
            pltpu.VMEM((devices, 1, pair_rows), jnp.float32),
            pltpu.VMEM((chunks, 2 * width, pair_rows), jnp.bfloat16),
            pltpu.VMEM((row_total, depth), jnp.bfloat16),
            pltpu.VMEM((blocks + 2, snp_rows, width), jnp.bfloat16),
            pltpu.VMEM((chunks + 1, snp_rows, 2 * width), jnp.bfloat16),
            pltpu.SemaphoreType.DMA((5,)),
            pltpu.SemaphoreType.DMA((chunks,)),
            pltpu.SemaphoreType.DMA((2,)),
            pltpu.SemaphoreType.DMA((4,)),
            pltpu.SemaphoreType.DMA((devices, parts)),
            pltpu.SemaphoreType.DMA((rounds + 1, chunks)),
            pltpu.SemaphoreType.DMA((rounds + 1, 2)),
        ],
        compiler_params=pltpu.CompilerParams(
            collective_id=0, has_side_effects=True, vmem_limit_bytes=EXCHANGE_LIMIT
        ),
    )(*[pltpu.with_memory_space_constraint(operand, pltpu.HBM) for operand in operands])


def put_kernel(source, target, done):
    copies = [
        pltpu.make_async_copy(
            source.at[pl.ds(index, 3)], target.at[pl.ds(index, 3)], done.at[index]
        )
        for index in range(0, source.shape[0], 3)
    ]
    for copy in copies:
        copy.start()
    for copy in copies:
        copy.wait()


def put_out(array):
    return pl.pallas_call(
        put_kernel,
        out_shape=jax.ShapeDtypeStruct(array.shape, array.dtype),
        in_specs=[pl.BlockSpec(memory_space=pl.ANY)],
        out_specs=pl.BlockSpec(memory_space=pl.ANY),
        scratch_shapes=[pltpu.SemaphoreType.DMA((array.shape[0],))],
        compiler_params=pltpu.CompilerParams(vmem_limit_bytes=PUT_LIMIT),
    )(array)


def per_device(eig_vectors, eig_values, eig_count, snp_count, zscores, samples):
    devices = lax.axis_size("panel")
    spacing = max(1, devices // 32)
    panels = devices // spacing
    slot_index = lax.axis_index("panel")
    panel_index = slot_index // spacing
    group_index = slot_index % spacing
    blocks_here, snp_rows, panel_width = zscores.shape[1:]
    if spacing == 1 and panels == 2 * ROUNDS and blocks_here == panels // 2:
        return put_out(
            exchange(eig_vectors, eig_values, samples, eig_count, snp_count, zscores)
        )
    counts = lax.dynamic_slice_in_dim(eig_count, group_index * blocks_here, blocks_here)
    snps = lax.dynamic_slice_in_dim(snp_count, group_index * blocks_here, blocks_here)
    rounds = jnp.arange(ROUNDS + 1, dtype=jnp.int32)
    partners = (panel_index - rounds) % panels
    scales = samples.astype(jnp.float32).reshape(panels, panel_width)
    own_scale = lax.dynamic_index_in_dim(scales, panel_index, 0, keepdims=False)
    scale = 1.0 / jnp.sqrt(own_scale[None, :, None] * scales[partners][:, None, :])
    members = [[g + spacing * i for i in range(panels)] for g in range(spacing)]
    gather = functools.partial(
        lax.all_gather, axis_name="panel", axis_index_groups=members if spacing > 1 else None
    )
    vectors = gather(eig_vectors, tiled=True)
    values = gather(eig_values, tiled=True)
    projected = project(vectors, zscores, counts, snps)
    held = gather(projected)
    weighted = (projected.astype(jnp.float32) / values.astype(jnp.float32)[:, None]).astype(
        jnp.bfloat16
    )
    return grams(weighted, held, scale, partners, counts)


def solution(mesh):
    placed = (
        P(("groups", "panel"), None),
        P(("groups", "panel")),
        P("groups"),
        P("groups"),
        P(("groups", "panel"), None, None, None),
        P("groups"),
    )
    return jax.shard_map(
        per_device,
        mesh=mesh,
        in_specs=placed,
        out_specs=P(None, ("groups", "panel"), None, None, None),
        check_vma=False,
    )
```

```python
import functools

import jax
import jax.numpy as jnp
from jax import lax
from jax.experimental import pallas as pl
from jax.experimental.pallas import tpu as pltpu
from jax.sharding import PartitionSpec as P

ROUNDS = 8
LIMIT = 56 * 1024 * 1024
EXCHANGE_LIMIT = 36 * 1024 * 1024
PUT_LIMIT = 1024 * 1024


def place_masked(snps, scores, pair, store):
    width = scores.shape[-1]
    for side in range(2):
        block = 2 * pair + side
        rows = lax.broadcasted_iota(jnp.int32, scores.shape[-2:], 0)
        part = jnp.where(rows < snps[block], scores[side].astype(jnp.float32), 0.0)
        store[:, side * width : (side + 1) * width] = part.astype(jnp.bfloat16)


def project_rows(vectors, masked, first_count):
    both = jnp.dot(vectors, masked, preferred_element_type=jnp.float32)
    width = both.shape[1] // 2
    rows = lax.broadcasted_iota(jnp.int32, (both.shape[0], width), 0)
    return jnp.where(rows < first_count, both[:, :width], both[:, width:]).astype(jnp.bfloat16)


def project_kernel(counts, snps, vectors, scores, out, masked):
    pair = pl.program_id(0)
    place_masked(snps, scores.at[0], pair, masked)
    out[...] = project_rows(vectors[...], masked[...], counts[2 * pair])


def project(vectors, scores, counts, snps):
    row_total, depth = vectors.shape
    blocks, snp_rows, width = scores.shape[1:]
    pair_rows = 2 * row_total // blocks
    return pl.pallas_call(
        project_kernel,
        out_shape=jax.ShapeDtypeStruct((row_total, width), jnp.bfloat16),
        grid_spec=pltpu.PrefetchScalarGridSpec(
            num_scalar_prefetch=2,
            grid=(blocks // 2,),
            in_specs=[
                pl.BlockSpec((pair_rows, depth), lambda b, *_: (b, 0)),
                pl.BlockSpec((1, 2, snp_rows, width), lambda b, *_: (0, b, 0, 0)),
            ],
            out_specs=pl.BlockSpec((pair_rows, width), lambda b, *_: (b, 0)),
            scratch_shapes=[pltpu.VMEM((snp_rows, 2 * width), jnp.bfloat16)],
        ),
        compiler_params=pltpu.CompilerParams(vmem_limit_bytes=LIMIT),
    )(counts, snps, vectors, scores)


def gram_kernel(counts, slots, weighted, panels, scale, out):
    pair = pl.program_id(0)
    width = weighted.shape[1]
    left = weighted[...].astype(jnp.float32)
    rows = lax.broadcasted_iota(jnp.int32, left.shape, 0)
    first = rows < counts[2 * pair]
    left = jnp.concatenate([jnp.where(first, left, 0.0).T, jnp.where(first, 0.0, left).T], axis=0)
    left = left.astype(jnp.bfloat16)
    shape = (width, width)
    same = lax.broadcasted_iota(jnp.int32, shape, 0) == lax.broadcasted_iota(jnp.int32, shape, 1)
    for index in range(out.shape[0]):
        both = jnp.dot(left, panels[slots[index]], preferred_element_type=jnp.float32)
        for side in range(2):
            gram = both[side * width : (side + 1) * width]
            if index == 0:
                count = counts[2 * pair + side].astype(jnp.float32)
                gram = gram - jnp.where(same, count, 0.0)
            out[index, 0, side] = gram * scale[index]


def grams(weighted, panels, scale, slots, counts):
    blocks = counts.shape[0]
    rounds, width = scale.shape[:2]
    pair_rows = 2 * weighted.shape[0] // blocks
    return pl.pallas_call(
        gram_kernel,
        out_shape=jax.ShapeDtypeStruct((rounds, 1, blocks, width, width), jnp.float32),
        grid_spec=pltpu.PrefetchScalarGridSpec(
            num_scalar_prefetch=2,
            grid=(blocks // 2,),
            in_specs=[
                pl.BlockSpec((pair_rows, width), lambda b, *_: (b, 0)),
                pl.BlockSpec((panels.shape[0], pair_rows, width), lambda b, *_: (0, b, 0)),
                pl.BlockSpec(scale.shape, lambda b, *_: (0, 0, 0)),
            ],
            out_specs=pl.BlockSpec((rounds, 1, 2, width, width), lambda b, *_: (0, 0, b, 0, 0)),
        ),
        compiler_params=pltpu.CompilerParams(vmem_limit_bytes=LIMIT),
    )(counts, slots, weighted, panels, scale)


def exchange_kernel(all_counts, all_snps, own, own_values, samples, scores, out, counts, snps,
                    flat_values, units, scale, held, values, left, store, raw, masked, here, load, shipped,
                    sent, recv1, recv4, recv2, recv3):
    line = lax.axis_size("panel") // 4
    me = lax.axis_index("panel")
    z = me // 4
    y = (me // 2) % 2
    k = me % 2
    piece = own.shape[0]
    pair_rows = 4 * piece
    parts = recv1.shape[1]
    part_rows = piece // (parts - 1)
    chunks = recv2.shape[1]
    top = line - 1
    fine = top
    inner = (z > 0) & (z < top)
    edge = (z == 0) | (z == top)
    up, down, across, beside = me + 4, me - 4, me + 2 - 4 * y, me + 1 - 2 * k
    inward = jnp.where(z == 0, up, down)
    outward = jnp.where(z == 1, down, up)
    pending = []
    pieces = []

    def order(plane, step):
        near = jnp.minimum(plane, top - plane)
        nearest = jnp.where(step > 2 * near, step, (near + (step + 1) // 2 * (1 - 2 * (step % 2))))
        return jnp.where(plane > top - plane, top - nearest, nearest)

    loads = []
    for step in range(line):
        pair = pl.ds(2 * order(z, step), 2)
        loads.append(
            pltpu.make_async_copy(scores.at[0, pair], raw.at[pl.ds(2 * step, 2)], load.at[step])
        )
    local = [
        pltpu.make_async_copy(own, store.at[pl.ds(me * piece, piece)], here.at[0]),
        pltpu.make_async_copy(own_values, flat_values, here.at[1]),
        pltpu.make_async_copy(all_counts, counts, here.at[2]),
        pltpu.make_async_copy(all_snps, snps, here.at[3]),
        pltpu.make_async_copy(samples, units, here.at[4]),
    ]
    barrier = pltpu.get_barrier_semaphore()

    def greet(target):
        pl.semaphore_signal(
            barrier, inc=1, device_id={"panel": target}, device_id_type=pl.DeviceIdType.MESH
        )

    pl.when(z < top)(functools.partial(greet, up))
    pl.when(z > 0)(functools.partial(greet, down))
    for target in (across, beside):
        greet(target)
    for copy in local + loads:
        copy.start()
    spot = lax.broadcasted_iota(jnp.int32, (piece, pair_rows), 1) - lax.rem(me, 4) * piece
    hot = jnp.where(spot == lax.broadcasted_iota(jnp.int32, spot.shape, 0), 1.0, 0.0)
    hot = hot.astype(jnp.bfloat16)
    pl.semaphore_wait(barrier, jnp.where(inner, 4, 3))

    def start(condition, copy, group=None):
        if condition is None:
            copy.start()
        else:
            pl.when(condition)(copy.start)
        (pending if group is None else group).append((condition, copy))

    def drain(group):
        for condition, copy in group:
            wait(condition, copy.wait_send)
        group.clear()

    def remote(source, target, send, recv, device):
        return pltpu.make_async_remote_copy(
            src_ref=source,
            dst_ref=target,
            send_sem=send,
            recv_sem=recv,
            device_id={"panel": device},
            device_id_type=pl.DeviceIdType.MESH,
        )

    def move1(source, part, way, target, first=False):
        arrival = recv1.at[source // 2, part]
        if way == 3:
            arrival = recv4.at[source // 2, part // (parts - 1)]
        sems = sent.at[0], arrival
        if part == parts - 1:
            return remote(values.at[source], values.at[source], *sems, target)
        rows = pl.ds(source * piece + part * part_rows, part_rows)
        origin = own.at[pl.ds(part * part_rows, part_rows)] if first else store.at[rows]
        return remote(origin, store.at[rows], *sems, target)

    def arrive1(source, part):
        move1(source, part, 0, me).wait_recv()

    def arrive_beside(source, some):
        if len(some) > 1:
            rows = store.at[pl.ds(source * piece, piece)]
            remote(rows, rows, sent.at[0], recv4.at[source // 2, 0], me).wait_recv()
        move1(source, parts - 1, 3, me).wait_recv()

    def slot(source, target):
        return jnp.minimum(lax.rem(target - source + 4 * line, 4 * line), recv2.shape[0] - 1)

    def move2(source, chunk, way, target, sends=1):
        block = held.at[source, pl.ds(chunk * pair_rows, pair_rows)]
        return remote(block, block, sent.at[sends], recv2.at[slot(source, target), chunk], target)

    def half2(step, source, chunk, half, target):
        rows = pl.ds(chunk * pair_rows + half * (pair_rows // 2), pair_rows // 2)
        block = held.at[source, rows]
        place = slot(source, target)
        arrival = recv3.at[place, step - fine] if half else recv2.at[place, chunk]
        return remote(block, block, sent.at[1], arrival, target)

    def give2(step, condition, source, chunk, target, some=range(2)):
        if step < fine:
            start(condition, move2(source, chunk, 0, target, 3), pieces)
        else:
            for half in some:
                start(condition, half2(step, source, chunk, half, target))

    def take2(step, condition, source, chunk, onward=()):
        if step < fine:
            wait(condition, arrive2, source, chunk)
            for where, target in onward:
                give2(step, where, source, chunk, target)
        else:
            for half in range(2):
                wait(condition, half2(step, source, chunk, half, me).wait_recv)
                for where, target in onward:
                    give2(step, where, source, chunk, target, [half])

    def arrive2(source, chunk):
        move2(source, chunk, 0, me).wait_recv()

    def both(a, b):
        return b if a is None else a & b

    def column(step, condition, some=None):
        plane = order(z, step)
        source = plane * 4 + y * 2 + k
        for part in range(parts) if some is None else some:
            wait(condition, arrive1, source, part)
            if step < top or part == parts - 1:
                start(condition & (plane < z) & (z < top), move1(source, part, 0, up), pieces)
                held_back = (z == 2) if step == 1 and part > 0 else (z < 0)
                start(condition & (plane > z) & (z > 0) & ~held_back, move1(source, part, 1, down), pieces)
            if step == 1:
                start(condition & edge, move1(source, part, 2, across), pieces)
            else:
                start(condition, move1(source, part, 2, across), pieces)
            start(condition, move1(source, part, 3, beside), pieces)

    def column_rest():
        for part in range(1, parts):
            start(z == 2, move1(me + 4, part, 1, down), pieces)

    def passing(step, condition):
        source = me + 4
        take2(step, condition, source, order(z + 1, step), [(condition, down)])

    def sideways(step, condition=None, some=None):
        source = order(z, step) * 4 + 2 - 2 * y + k
        for part in range(parts) if some is None else some:
            wait(condition, arrive1, source, part)
            start(condition, move1(source, part, 3, beside), pieces)
            if step == 0:
                start(both(condition, edge), move1(source, part, 0, inward), pieces)

    def mask(step):
        loads[step].wait()
        place_masked(snps, raw.at[pl.ds(2 * step, 2)], order(z, step), masked.at[step])

    def wait(condition, arrive, *where):
        if condition is None:
            arrive(*where)
        else:
            pl.when(condition)(functools.partial(arrive, *where))

    def beside_pieces(step, condition, some):
        plane = order(z, step)
        for source in (plane * 4 + y * 2 + 1 - k, plane * 4 + 2 - 2 * y + 1 - k):
            wait(condition, arrive_beside, source, some)

    def compute(step):
        plane = order(z, step)
        rows = pl.ds(plane * pair_rows, pair_rows)
        held[me, rows] = project_rows(store[rows], masked[step], counts[2 * plane])

    def finish(step, condition=None):
        plane = order(z, step)
        beside_pieces(step, condition, range(parts))
        wait(condition, compute, step)
        give2(step, both(condition, z < top), me, plane, up)
        give2(step, (z == 2) if step == top else (z >= 2), me, plane, down)
        start(both(condition, k == 0), move2(me, plane, 3, beside))
        wait(condition, weigh, plane)

    def ship(half):
        block = 2 * order(z, top) + half
        return remote(
            scores.at[0, pl.ds(block, 1)],
            raw.at[pl.ds(2 * line + half, 1)],
            sent.at[2],
            shipped.at[half],
            inward,
        )

    def compute_outside():
        plane = order(z, top)
        for half in range(2):
            ship(half).wait_recv()
        place_masked(snps, raw.at[pl.ds(2 * line, 2)], plane, masked.at[line])
        rows = pl.ds(plane * pair_rows, pair_rows)
        held[outward, rows] = project_rows(store[rows], masked[line], counts[2 * plane])

    def outside():
        plane = order(z, top)
        pl.when(inner)(compute_outside)
        for half in range(2):
            give2(top, inner, outward, plane, up, [half])
            give2(top, inner & ~late_return, outward, plane, down, [half])
            give2(top, z == 1, outward, plane, across, [half])
        start(z == 1, move2(outward, plane, 3, beside))

    late_return = (z == 1) & (y == 1)

    def outside_rest():
        give2(top, late_return, outward, order(z, top), down)

    def returned(condition):
        plane = order(z, top)
        beside_pieces(top, condition, [parts - 1])
        take2(top, condition, me, plane, [(condition & (y == 0), across)])
        start(condition & (k == 0), move2(me, plane, 3, beside))
        wait(condition, weigh, plane)

    def weigh(index):
        rows = pl.ds(index * pair_rows, pair_rows)
        row = values[4 * index] + values[4 * index + 1]
        row = row + (values[4 * index + 2] + values[4 * index + 3])
        flat = held[me, rows].astype(jnp.float32).T / row
        first = lax.broadcasted_iota(jnp.int32, flat.shape, 1) < counts[2 * index]
        both = jnp.concatenate([jnp.where(first, flat, 0.0), jnp.where(first, 0.0, flat)], axis=0)
        left[index] = both.astype(jnp.bfloat16)

    def scales():
        table = units[...].astype(jnp.float32)
        panels = lax.broadcasted_iota(jnp.int32, table.shape, 0)

        def row(panel):
            return jnp.sum(jnp.where(panels == panel, table, 0.0), axis=0, keepdims=True)

        width = table.shape[1]
        mine = jnp.broadcast_to(row(me), (width, width)).T
        for number in range(out.shape[0]):
            partner = lax.rem(me - number + 4 * line, 4 * line)
            scale[number] = 1.0 / jnp.sqrt(mine * row(partner))

    def plane_behind(lag):
        return lax.rem(z - lag + line, line)

    def own_across(step, condition=None):
        give2(step, both(condition, y == 0), me, order(z, step), across)

    def relay(step, turn, condition=None):
        lag = jnp.where(z == 0, 2 - turn, 1 + turn)
        plane = plane_behind(lag)
        source = plane * 4 + y * 2 + k
        chunk = order(plane, step)
        onward = [
            (both(condition, (lag == 1) & inner), up),
            (both(condition, (lag == 2) & (z == 1)), down),
            (both(condition, (lag == 1) | (y == 1)), across),
        ]
        take2(step, condition, source, chunk, onward)
        start(both(condition, (lag == 1) | (k == 1)), move2(source, chunk, 3, beside))

    cross = [plane_behind(lag + 1 - y) * 4 + (1 - y) * 2 + k for lag in range(2)]
    swap = 1 - 2 * k

    def cross_over(step):
        for source in cross:
            chunk = order(source // 4, step)
            take2(step, None, source, chunk)
            start(None, move2(source, chunk, 3, beside))

    def turn_of(source, place):
        plane = source // 4
        late = sum(jnp.where(order(plane, step) == order(z, top), step, 0) for step in range(line))
        if place == 2:
            step = late
        else:
            rank = min(place, 2)
            step = rank + jnp.where(rank >= late, 1, 0)
        return order(plane, jnp.where(edge, step, place))

    def gram(source, step, number, own_panel=False):
        chunk = turn_of(source, step)
        rows = pl.ds(chunk * pair_rows, pair_rows)
        both = jnp.dot(left[chunk], held[source, rows], preferred_element_type=jnp.float32)
        width = both.shape[1]
        for side in range(2):
            part = both[side * width : (side + 1) * width]
            if own_panel:
                shape = (width, width)
                across_rows = lax.broadcasted_iota(jnp.int32, shape, 0)
                same = across_rows == lax.broadcasted_iota(jnp.int32, shape, 1)
                count = counts[2 * chunk + side].astype(jnp.float32)
                part = part - jnp.where(same, count, 0.0)
            out[number, 0, 2 * chunk + side] = part * scale[number]

    def lag_of(turn):
        return turn if turn == 0 else jnp.where(z == 0, 3 - turn, turn)

    def near_gram(turn, *places, condition=None):
        lag = lag_of(turn)
        source = plane_behind(lag) * 4 + y * 2 + k
        for place in places:
            wait(condition, gram, source, place, 4 * lag, turn == 0)

    def near_beside(turn, *places, condition=None):
        lag = lag_of(turn)
        number = 4 * lag - swap
        source = plane_behind(lag) * 4 + y * 2 + 1 - k
        for place in places:

            @pl.when(both(condition, (number >= 0) & (number < out.shape[0])))
            def _():
                arrive2(source, turn_of(source, place))
                gram(source, place, number)

    def cross_gram(*places, condition=None):
        for place in places:
            for lag, source in enumerate(cross):
                wait(condition, gram, source, place, 4 * lag + 2)

    def cross_beside(*places, condition=None):
        def beside_gram(source, place, number):
            arrive2(source, turn_of(source, place))
            gram(source, place, number)

        for place in places:
            for lag, source in enumerate(cross):
                wait(condition, beside_gram, source + swap, place, 4 * lag + 2 - swap)

    for part in range(parts):
        if part == parts - 1:
            for copy in local[1:]:
                copy.wait()
            ride = flat_values[...].astype(jnp.float32).reshape(1, piece)
            ride = jnp.broadcast_to(ride, (8, piece)).astype(jnp.bfloat16)
            values[me] = jnp.dot(ride, hot, preferred_element_type=jnp.float32)[0:1]
        start(z < top, move1(me, part, 0, up, True), pieces)
        start(z > 0, move1(me, part, 1, down, True), pieces)
        start(None, move1(me, part, 2, across, True), pieces)
        start(None, move1(me, part, 3, beside, True), pieces)
    mask(0)
    local[0].wait()
    mask(1)
    mask(2)
    mask(3)
    scales()
    for some in ([0], list(range(1, parts))):
        column(1, inner, some)
        column(2, inner, some)
        column(1, edge, some)
        sideways(0, edge, some)
    sideways(0, inner)
    finish(0)
    column_rest()
    column(2, edge)
    column(3, inner, [0])
    passing(0, z == 1)
    sideways(1, z == 1)
    column(3, inner, [1, 2])
    sideways(1, z != 1)
    finish(1)
    start(edge, ship(0))
    own_across(0)
    passing(1, z == 1)
    relay(0, 0, inner)
    passing(0, z == 2)
    sideways(2)
    finish(2)
    start(edge, ship(1))
    passing(1, z == 2)
    relay(1, 0, z == 2)
    relay(0, 0, edge)
    column(3, edge, [parts - 1])
    sideways(3, inner)
    relay(0, 1, z == 1)
    finish(3, inner)
    own_across(1)
    relay(0, 1, z == 2)
    near_gram(0, 0, 1, 3)
    relay(1, 0, edge)
    passing(2, inner)
    relay(1, 0, z == 1)
    near_beside(0, 0, 1, 3)
    relay(0, 1, edge)
    near_gram(1, 0)
    relay(2, 0, z == 2)
    relay(1, 1, z == 1)
    relay(2, 0, z == 1)
    relay(2, 0, edge)
    near_gram(1, 1)
    near_beside(1, 0)
    passing(3, (z == 1) & (y == 1))
    own_across(2)
    outside()
    relay(3, 0, z == 2)
    near_beside(1, 1)
    relay(1, 1, edge)
    near_gram(2, 0)
    relay(2, 1, z == 1)
    relay(1, 1, z == 2)
    near_beside(2, 0)
    relay(3, 0, (z == 3) | ((z == 0) & (y == 1)))
    cross_over(0)
    sideways(3, edge, [parts - 1])
    own_across(3, inner)
    relay(3, 1, z == 1)
    passing(3, (z == 1) & (y == 0))
    outside_rest()
    relay(2, 1, z == 2)
    relay(3, 1, z == 2)
    relay(2, 1, z == 3)
    returned((z == 3) | ((z == 0) & (y == 0)))
    cross_over(1)
    cross_gram(0)
    relay(2, 1, z == 0)
    cross_beside(0)
    near_gram(2, 1)
    near_beside(2, 1)
    relay(3, 1, edge)
    near_gram(2, 3)
    last_return = (z == 0) & (y == 1)
    for turn in range(3):
        near_gram(turn, 2, condition=~last_return)
    for turn in range(3):
        near_beside(turn, 2, condition=~last_return)
    drain(pieces)
    cross_over(2)
    cross_gram(1)
    near_beside(2, 3)
    relay(3, 0, (z == 0) & (y == 0))
    near_gram(1, 3)
    cross_beside(1)
    returned(last_return)
    for turn in range(3):
        near_gram(turn, 2, condition=last_return)
    for turn in range(3):
        near_beside(turn, 2, condition=last_return)
    early = inner | ((z == 0) & (y == 0))
    cross_gram(2, condition=early)
    cross_over(3)
    cross_gram(2, condition=~early)
    cross_beside(2)
    cross_gram(3)
    near_beside(1, 3)
    cross_beside(3)
    drain(pending)


def exchange(vectors, values, samples, counts, snps, scores):
    devices = lax.axis_size("panel")
    piece, depth = vectors.shape
    blocks, snp_rows, width = scores.shape[1:]
    row_total = devices * piece
    pair_rows = 4 * piece
    parts = 3
    chunks = blocks // 2
    rounds = ROUNDS + 1
    hbm = pl.BlockSpec(memory_space=pltpu.HBM)
    operands = [counts, snps, vectors, values, samples.reshape(devices, width), scores]
    return pl.pallas_call(
        exchange_kernel,
        out_shape=jax.ShapeDtypeStruct((rounds, 1, blocks, width, width), jnp.float32),
        in_specs=[hbm] * len(operands),
        out_specs=pl.BlockSpec(memory_space=pltpu.VMEM),
        scratch_shapes=[
            pltpu.SMEM((blocks,), jnp.int32),
            pltpu.SMEM((blocks,), jnp.int32),
            pltpu.VMEM((piece,), jnp.bfloat16),
            pltpu.VMEM((devices, width), jnp.bfloat16),
            pltpu.VMEM((rounds, width, width), jnp.float32),
            pltpu.VMEM((devices, row_total, width), jnp.bfloat16),
            pltpu.VMEM((devices, 1, pair_rows), jnp.float32),
            pltpu.VMEM((chunks, 2 * width, pair_rows), jnp.bfloat16),
            pltpu.VMEM((row_total, depth), jnp.bfloat16),
            pltpu.VMEM((blocks + 2, snp_rows, width), jnp.bfloat16),
            pltpu.VMEM((chunks + 1, snp_rows, 2 * width), jnp.bfloat16),
            pltpu.SemaphoreType.DMA((5,)),
            pltpu.SemaphoreType.DMA((chunks,)),
            pltpu.SemaphoreType.DMA((2,)),
            pltpu.SemaphoreType.DMA((4,)),
            pltpu.SemaphoreType.DMA((devices // 2, parts)),
            pltpu.SemaphoreType.DMA((devices // 2, 2)),
            pltpu.SemaphoreType.DMA((rounds + 1, chunks)),
            pltpu.SemaphoreType.DMA((rounds + 1, 1)),
        ],
        compiler_params=pltpu.CompilerParams(
            collective_id=0, has_side_effects=True, vmem_limit_bytes=EXCHANGE_LIMIT
        ),
    )(*[pltpu.with_memory_space_constraint(operand, pltpu.HBM) for operand in operands])


def put_kernel(source, target, done):
    copies = [
        pltpu.make_async_copy(
            source.at[pl.ds(index, 3)], target.at[pl.ds(index, 3)], done.at[index]
        )
        for index in range(0, source.shape[0], 3)
    ]
    for copy in copies:
        copy.start()
    for copy in copies:
        copy.wait()


def put_out(array):
    return pl.pallas_call(
        put_kernel,
        out_shape=jax.ShapeDtypeStruct(array.shape, array.dtype),
        in_specs=[pl.BlockSpec(memory_space=pl.ANY)],
        out_specs=pl.BlockSpec(memory_space=pl.ANY),
        scratch_shapes=[pltpu.SemaphoreType.DMA((array.shape[0],))],
        compiler_params=pltpu.CompilerParams(vmem_limit_bytes=PUT_LIMIT),
    )(array)


def per_device(eig_vectors, eig_values, eig_count, snp_count, zscores, samples):
    devices = lax.axis_size("panel")
    spacing = max(1, devices // 32)
    panels = devices // spacing
    slot_index = lax.axis_index("panel")
    panel_index = slot_index // spacing
    group_index = slot_index % spacing
    blocks_here, snp_rows, panel_width = zscores.shape[1:]
    if spacing == 1 and panels == 2 * ROUNDS and blocks_here == panels // 2:
        return put_out(
            exchange(eig_vectors, eig_values, samples, eig_count, snp_count, zscores)
        )
    counts = lax.dynamic_slice_in_dim(eig_count, group_index * blocks_here, blocks_here)
    snps = lax.dynamic_slice_in_dim(snp_count, group_index * blocks_here, blocks_here)
    rounds = jnp.arange(ROUNDS + 1, dtype=jnp.int32)
    partners = (panel_index - rounds) % panels
    scales = samples.astype(jnp.float32).reshape(panels, panel_width)
    own_scale = lax.dynamic_index_in_dim(scales, panel_index, 0, keepdims=False)
    scale = 1.0 / jnp.sqrt(own_scale[None, :, None] * scales[partners][:, None, :])
    members = [[g + spacing * i for i in range(panels)] for g in range(spacing)]
    gather = functools.partial(
        lax.all_gather, axis_name="panel", axis_index_groups=members if spacing > 1 else None
    )
    vectors = gather(eig_vectors, tiled=True)
    values = gather(eig_values, tiled=True)
    projected = project(vectors, zscores, counts, snps)
    held = gather(projected)
    weighted = (projected.astype(jnp.float32) / values.astype(jnp.float32)[:, None]).astype(
        jnp.bfloat16
    )
    return grams(weighted, held, scale, partners, counts)


def solution(mesh):
    placed = (
        P(("groups", "panel"), None),
        P(("groups", "panel")),
        P("groups"),
        P("groups"),
        P(("groups", "panel"), None, None, None),
        P("groups"),
    )
    return jax.shard_map(
        per_device,
        mesh=mesh,
        in_specs=placed,
        out_specs=P(None, ("groups", "panel"), None, None, None),
        check_vma=False,
    )
```
